512 devices in a mesh: space: 64 (over y, x, core), chan: 8 (over z).
Axes of the slice: x: 4, y: 8, z: 8, core: 2. Of those that a mesh axis runs over, the one named last changes fastest.
Arguments:
- features: bfloat16 [65536, 256], P('space', 'chan'), may hold values from -6 to 6
- weights: bfloat16 [27, 256, 256], P(None, 'chan'), may hold values from -0.125 to 0.125
- send_rows: int32 [64, 8, 768], P('space'), may hold values from 0 to 1024, as said below
- gather_map: int32 [27, 65536], P(None, 'space'), may hold values from 0 to 7168, as said below
Outputs:
- output: bfloat16 [65536, 256], P('space', 'chan')
The draws below stay inside these ranges and needn't reach their ends.
Inputs may be any that keep to these rules, and one draw needn't show every extreme that they name: `send_rows`: an entry of 1024 marks an empty slot; the others are local row numbers of the sending block. Every direction of every block has some empty slots. `gather_map`: an entry of 7168 names the zero row; offset 13 (the centre) maps each voxel to its own local row.
All inputs are finite; a program needn't handle non-finite values.
Results may differ from the reference program's by a relative error of at most 0.001.
Values may be sent and summed in bfloat16 or wider, within the bound.
No kernel may reach another device: no remote copies, remote signals or barrier semaphores. Data moves between devices by JAX's collectives and lax.ppermute only.
A program may use at most 64 MiB of HBM per device.

```python
import jax
import jax.numpy as jnp
from jax import lax

C = 256
OFFSETS = 27
GRID_COLS = 8
V_DEV = 1024
HALO = 768
BLOCKS = 64
VOX = 65536


def draw_send_rows(key, part):
    first, second = jax.random.split(jax.random.fold_in(key, 11))
    counts = jax.random.randint(first, (BLOCKS, 8, 1), HALO // 4, HALO)
    local_rows = jax.random.randint(second, (BLOCKS, 8, HALO), 0, V_DEV)
    slot = jnp.arange(HALO, dtype=jnp.int32)[None, None, :]
    return jnp.where(slot < counts, local_rows, V_DEV).astype(jnp.int32)


def draw_gather_map(key, part):
    first, second, third = jax.random.split(jax.random.fold_in(key, 23), 3)
    kind_of = jax.random.randint(first, (OFFSETS, VOX), 0, 4)
    local_rows = jax.random.randint(second, (OFFSETS, VOX), 0, V_DEV)
    remote_rows = V_DEV + jax.random.randint(third, (OFFSETS, VOX), 0, 8 * HALO)
    empty_row = V_DEV + 8 * HALO
    picked = jnp.where(kind_of < 2, local_rows, jnp.where(kind_of == 2, remote_rows, empty_row))
    own_rows = (jnp.arange(VOX, dtype=jnp.int32) % V_DEV)[None, :]
    centre = (jnp.arange(OFFSETS, dtype=jnp.int32) == 13)[:, None]
    return jnp.where(centre, own_rows, picked).astype(jnp.int32)


def spiked(array, key, source, target, shards_of, factor):
    owner, partner = [(jnp.arange(array.shape[axis_at]) // (array.shape[axis_at] // shards_of)).reshape([-1 if axis == axis_at else 1 for axis in range(array.ndim)]) for axis_at in (source, target)]
    chosen = jax.random.permutation(key, shards_of)[partner]
    strong = (owner == chosen) | (owner == (partner + shards_of // 2) % shards_of)
    return jnp.where(strong, factor * array, array)


def shard_levels(stream_key, extent, cuts, least, largest):
    level = 1.0
    for dim, shards_of in cuts:
        draws = jax.random.uniform(jax.random.fold_in(jax.random.fold_in(stream_key, 6), dim), (shards_of,), jnp.float32, least / len(cuts), largest / len(cuts))
        level = level * jnp.repeat(jnp.exp(draws), extent[dim] // shards_of).reshape((-1,) + (1,) * (len(extent) - 1 - dim))
    return level


def centred(key, shape, spread, limit, cuts=(), held_as=jnp.bfloat16):
    drawn = jax.random.normal(key, shape, jnp.float32) * spread
    if len(cuts) > 0:
        drawn = shard_levels(key, shape, cuts, -0.22, 0.18) * drawn
    return jnp.clip(drawn, min=-limit, max=limit).astype(held_as)


def gaussian_with(own_key, dims, scale, reach, cuts, heavy, kind=jnp.bfloat16):
    values = scale * jax.random.normal(own_key, dims, jnp.float32)
    if cuts:
        values = values * shard_levels(own_key, dims, cuts, -0.22, 0.18)
    return jnp.clip(spiked(values, jax.random.fold_in(own_key, 3), *heavy), -reach, reach).astype(kind)


def setup_inputs(seed: int = 0) -> dict:
    splits = jax.random.split(jax.random.key(seed), 5)
    features = centred(splits[0], (VOX, C), 1.0, 6.0, ((0, 64), (1, 8)))
    weights = gaussian_with(splits[1], (OFFSETS, C, C), (14 * C) ** -0.5, 0.125, ((1, 8),), (1, 2, 8, 2.0))
    send_rows = draw_send_rows(jax.random.fold_in(splits[4], 71), 0)
    gather_map = draw_gather_map(jax.random.fold_in(splits[4], 71), 0)
    return {"features": features, "weights": weights, "send_rows": send_rows, "gather_map": gather_map}


directions = [(-1, -1), (-1, 0), (-1, 1), (0, -1), (0, 1), (1, -1), (1, 0), (1, 1)]


def reference(features, weights, send_rows, gather_map):
    grid_rows = BLOCKS // GRID_COLS
    blocked = features.reshape(BLOCKS, V_DEV, C)
    padded = jnp.concatenate([blocked, jnp.zeros((BLOCKS, 1, C), jnp.bfloat16)], axis=1)
    kernel = weights.astype(jnp.float32)

    def one_block(block):
        block_row = block // GRID_COLS
        block_col = block % GRID_COLS
        pieces = [padded[block, :V_DEV]]
        for number, (step_x, step_y) in enumerate(directions):
            src_row = block_row - step_x
            src_col = block_col - step_y
            inside = (src_row >= 0) & (src_row < grid_rows) & (src_col >= 0) & (src_col < GRID_COLS)
            source = jnp.clip(src_row * GRID_COLS + src_col, 0, BLOCKS - 1).astype(jnp.int32)
            wanted = send_rows[source, number]
            got = padded[source][wanted]
            pieces.append(jnp.where(inside, got, jnp.zeros_like(got)))
        pieces.append(jnp.zeros((1, C), jnp.bfloat16))
        table = jnp.concatenate(pieces, axis=0)
        index = lax.dynamic_slice_in_dim(gather_map, (block * V_DEV).astype(jnp.int32), V_DEV, 1)
        picked = table[index].astype(jnp.float32)
        total = jnp.einsum("kvc,kco->vo", picked, kernel)
        return total.astype(jnp.bfloat16)

    result = lax.map(one_block, jnp.arange(BLOCKS, dtype=jnp.int32))
    return result.reshape(VOX, C)
```

```python
import jax
import jax.numpy as jnp
from jax import lax
from jax.experimental import pallas as pl
from jax.experimental.pallas import tpu as pltpu
from jax.sharding import PartitionSpec as P

GRID = 8
V = 1024
HALF = V // 2
HALO = 768
OFFS = 27
PAIRS = 14
ZERO = 9 * V
ROWS = ZERO + 8
BLOCK_OF = (8, 2, 5, 6, 3, 7, 1, 4)


def shift(value, step_row, step_col):
    pairs = [
        (row * GRID + col, (row + step_row) * GRID + col + step_col)
        for row in range(GRID)
        for col in range(GRID)
        if 0 <= row + step_row < GRID and 0 <= col + step_col < GRID
    ]
    return lax.ppermute(value, "space", pairs)


def digits(rows):
    parts = []
    for row in rows:
        parts += [row >> 5, row & 31]
    table = jnp.stack(parts, axis=0).astype(jnp.bfloat16)
    return jnp.pad(table, ((0, 8 - len(parts)), (0, V - HALO)))


def conv_kernel(par_ref, gm_ref, own_ref, up_ref, dn_ref, xp_ref, xm_ref, w0_ref, w1_ref,
                out_ref, table, lut, comp, index, lhs, wall, sem):
    par = par_ref[0]
    sources = [own_ref.at[pl.ds(0, 72)], up_ref.at[pl.ds(0, 72)], dn_ref.at[pl.ds(0, 72)]]
    for ref in (xp_ref, xm_ref):
        sources += [ref.at[pl.ds(72 * i, 72)] for i in range(3)]

    for number, block in enumerate(BLOCK_OF):
        step_col = (-1, 0, 1, -1, 1, -1, 0, 1)[number]
        at = 2 * (step_col + 1)
        pieces = sources[block][64:72, :HALO].astype(jnp.float32)
        slot = (pieces[at:at + 1] * 32.0 + pieces[at + 1:at + 2]).astype(jnp.int32)
        slot = jnp.where(slot >= V, ZERO, slot + block * V)
        for j in range(HALO // 128):
            lut[6 * number + j:6 * number + j + 1, :] = slot[:, 128 * j:128 * (j + 1)]

    for k0 in range(0, 32, 8):
        rows = min(8, OFFS - k0)
        for c in range(HALF // 128):
            here = gm_ref[k0:k0 + rows, pl.ds(pl.multiple_of(par * HALF + 128 * c, 128), 128)]
            if rows < 8:
                here = jnp.concatenate([here, jnp.full((8 - rows, 128), 8 * HALO + V, jnp.int32)], axis=0)
            slot = here - V
            hi = lax.shift_right_arithmetic(slot, 7)
            lo = slot & 127
            got = jnp.where(slot < 0, here, ZERO)
            for t in range(8 * HALO // 128):
                line = jnp.broadcast_to(lut[t:t + 1, :], (8, 128))
                value = jnp.take_along_axis(line, lo, axis=1)
                got = jnp.where(hi == t, value, got)
            comp[k0:k0 + 8, 128 * c:128 * (c + 1)] = got
    copy = pltpu.make_async_copy(comp, index, sem)
    copy.start()

    for block, source in enumerate(sources):
        for c in range(V // 128):
            x = source[0:64, 128 * c:128 * (c + 1)].astype(jnp.float32)
            x = jnp.concatenate([x, x], axis=0)
            table[block * V + 128 * c:block * V + 128 * (c + 1), :] = x.T
    table[ZERO:ROWS, :] = jnp.zeros((8, 128), jnp.float32)

    for k in range(OFFS):
        for side, w_ref in ((par, w0_ref), (1 - par, w1_ref)):
            wall[pl.ds(pl.multiple_of(64 * k + 32 * side, 32), 32), :] = w_ref[32 * k:32 * k + 32, :]
    wall[64 * OFFS:, :] = jnp.zeros((64, 256), jnp.bfloat16)
    copy.wait()

    sub = lax.broadcasted_iota(jnp.int32, (8, 128), 0)
    lane = lax.broadcasted_iota(jnp.int32, (8, 128), 1)
    masks = [sub == j for j in range(8)]
    left = lane < 64

    for pair in range(PAIRS):
        @pl.loop(0, HALF // 32)
        def _(step):
            base = pl.multiple_of(step * 32, 32)
            tiles = []
            for g in range(4):
                sides = []
                for k in (2 * pair, 2 * pair + 1):
                    acc = None
                    for j in range(8):
                        if k >= OFFS:
                            acc = jnp.zeros((8, 128), jnp.float32)
                            continue
                        row = table[pl.ds(index[k, base + 8 * g + j], 8, stride=0), :]
                        acc = row if acc is None else jnp.where(masks[j], row, acc)
                    sides.append(acc)
                tiles.append(jnp.where(left, sides[0], sides[1]))
            lhs[pl.ds(base, 32), 128 * pair:128 * (pair + 1)] = jnp.concatenate(tiles, axis=0).astype(jnp.bfloat16)

    total = jnp.dot(lhs[...], wall[...], preferred_element_type=jnp.float32)
    out_ref[...] = total.T


def add_kernel(got_ref, out_ref):
    for half in range(2):
        total = got_ref[half]
        for p in range(1, 4):
            total = total + got_ref[2 * p + half]
        out_ref[HALF * half:HALF * (half + 1), :] = total.T.astype(jnp.bfloat16)


def local(features, weights, send_rows, gather_map):
    width = features.shape[1]
    par = lax.axis_index("chan") % 2
    flip = [(i, i ^ 1) for i in range(8)]
    duo = [[2 * i, 2 * i + 1] for i in range(4)]
    w0 = weights.reshape(OFFS * width, 256)
    both = lax.all_gather(features.T, "chan", axis=0, tiled=True, axis_index_groups=duo)
    rows = send_rows[0]
    own = jnp.concatenate([both, digits([rows[3], rows[3], rows[4]])], axis=0)
    to_up = jnp.concatenate([both, digits([rows[5], rows[6], rows[7]])], axis=0)
    to_dn = jnp.concatenate([both, digits([rows[0], rows[1], rows[2]])], axis=0)
    up = shift(to_up, 1, 0)
    dn = shift(to_dn, -1, 0)
    w1 = lax.ppermute(w0, "chan", flip)
    strip = jnp.concatenate([own, up, dn], axis=0)
    xp = shift(strip, 0, 1)
    xm = shift(strip, 0, -1)
    vmem = pl.BlockSpec(memory_space=pltpu.VMEM)
    part = pl.pallas_call(
        conv_kernel,
        out_shape=jax.ShapeDtypeStruct((256, HALF), jnp.float32),
        in_specs=[pl.BlockSpec(memory_space=pltpu.SMEM)] + [vmem] * 8,
        out_specs=vmem,
        scratch_shapes=[
            pltpu.VMEM((ROWS, 128), jnp.float32),
            pltpu.VMEM((48, 128), jnp.int32),
            pltpu.VMEM((32, HALF), jnp.int32),
            pltpu.SMEM((32, HALF), jnp.int32),
            pltpu.VMEM((HALF, 128 * PAIRS), jnp.bfloat16),
            pltpu.VMEM((128 * PAIRS, 256), jnp.bfloat16),
            pltpu.SemaphoreType.DMA,
        ],
        compiler_params=pltpu.CompilerParams(vmem_limit_bytes=40 * 2**20),
        name="conv",
    )(par.reshape(1).astype(jnp.int32), gather_map, own, up, dn, xp, xm, w0, w1)
    got = lax.all_to_all(part, "chan", 0, 0, tiled=True).reshape(8, 32, HALF)
    return pl.pallas_call(
        add_kernel,
        out_shape=jax.ShapeDtypeStruct((V, 32), jnp.bfloat16),
        in_specs=[vmem],
        out_specs=vmem,
        name="add",
    )(got)


def solution(mesh):
    in_specs = (P("space", "chan"), P(None, "chan", None), P("space", None, None), P(None, "space"))
    out_specs = P("space", "chan")
    return jax.shard_map(local, mesh=mesh, in_specs=in_specs, out_specs=out_specs, check_vma=False)
```

```python
import jax
import jax.numpy as jnp
from jax import lax
from jax.experimental import pallas as pl
from jax.experimental.pallas import tpu as pltpu
from jax.sharding import PartitionSpec as P

GRID = 8
V = 1024
HALF = V // 2
HALO = 768
OFFS = 27
PAIRS = 14
ZERO = 9 * V
ROWS = ZERO + 8
BLOCK_OF = (8, 2, 5, 6, 3, 7, 1, 4)


def shift(value, step_row, step_col):
    pairs = [
        (row * GRID + col, (row + step_row) * GRID + col + step_col)
        for row in range(GRID)
        for col in range(GRID)
        if 0 <= row + step_row < GRID and 0 <= col + step_col < GRID
    ]
    return lax.ppermute(value, "space", pairs)


def digits(rows):
    parts = []
    for row in rows:
        parts += [row >> 5, row & 31]
    table = jnp.stack(parts, axis=0).astype(jnp.bfloat16)
    return jnp.pad(table, ((0, 8 - len(parts)), (0, V - HALO)))


def conv_kernel(par_ref, gm_ref, own_ref, up_ref, dn_ref, xp_ref, xm_ref, w0_ref, w1_ref,
                out_ref, table, lut, comp, index, lhs, wall, sem):
    par = par_ref[0]
    sources = [own_ref.at[pl.ds(0, 72)], up_ref.at[pl.ds(0, 72)], dn_ref.at[pl.ds(0, 72)]]
    for ref in (xp_ref, xm_ref):
        sources += [ref.at[pl.ds(72 * i, 72)] for i in range(3)]

    for number, block in enumerate(BLOCK_OF):
        step_col = (-1, 0, 1, -1, 1, -1, 0, 1)[number]
        at = 2 * (step_col + 1)
        pieces = sources[block][64:72, :HALO].astype(jnp.float32)
        slot = (pieces[at:at + 1] * 32.0 + pieces[at + 1:at + 2]).astype(jnp.int32)
        slot = jnp.where(slot >= V, ZERO, slot + block * V)
        for j in range(HALO // 128):
            lut[6 * number + j:6 * number + j + 1, :] = slot[:, 128 * j:128 * (j + 1)]

    for k0 in range(0, 32, 8):
        rows = min(8, OFFS - k0)
        for c in range(HALF // 128):
            here = gm_ref[k0:k0 + rows, pl.ds(pl.multiple_of(par * HALF + 128 * c, 128), 128)]
            if rows < 8:
                here = jnp.concatenate([here, jnp.full((8 - rows, 128), 8 * HALO + V, jnp.int32)], axis=0)
            slot = here - V
            hi = lax.shift_right_arithmetic(slot, 7)
            lo = slot & 127
            got = jnp.where(slot < 0, here, ZERO)
            for t in range(8 * HALO // 128):
                line = jnp.broadcast_to(lut[t:t + 1, :], (8, 128))
                value = jnp.take_along_axis(line, lo, axis=1)
                got = jnp.where(hi == t, value, got)
            comp[32 * c + k0:32 * c + k0 + 8, :] = got
    copy = pltpu.make_async_copy(comp, index, sem)
    copy.start()

    for block, source in enumerate(sources):
        for c in range(V // 128):
            x = source[0:64, 128 * c:128 * (c + 1)].astype(jnp.float32)
            x = jnp.concatenate([x, x], axis=0)
            table[block * V + 128 * c:block * V + 128 * (c + 1), :] = x.T
    table[ZERO:ROWS, :] = jnp.zeros((8, 128), jnp.float32)

    for k in range(OFFS):
        for side, w_ref in ((par, w0_ref), (1 - par, w1_ref)):
            wall[pl.ds(pl.multiple_of(64 * k + 32 * side, 32), 32), :] = w_ref[32 * k:32 * k + 32, :]
    wall[64 * OFFS:, :] = jnp.zeros((64, 256), jnp.bfloat16)
    copy.wait()

    sub = lax.broadcasted_iota(jnp.int32, (8, 128), 0)
    lane = lax.broadcasted_iota(jnp.int32, (8, 128), 1)
    masks = [sub == j for j in range(8)]
    left = lane < 64

    def pick(step, last):
        pair = PAIRS - 1 if last else step >> 2
        quarter = step & 3
        line = quarter * 32 + 2 * pair
        for h in range(0, 128, 16):
            tiles = []
            for g in range(h, h + 16, 8):
                sides = []
                for side in range(1 if last else 2):
                    acc = None
                    for j in range(8):
                        at = index.at[pl.ds(side, 127), pl.ds(g + j, 1)][line, 0]
                        row = table[pl.ds(at, 8, stride=0), :]
                        acc = row if acc is None else jnp.where(masks[j], row, acc)
                    sides.append(acc)
                tiles.append(jnp.where(left, sides[0], 0.0 if last else sides[1]))
            rows = pl.ds(pl.multiple_of(quarter * 128 + h, 16), 16)
            lanes = pl.ds(pl.multiple_of(128 * pair, 128), 128)
            lhs[rows, lanes] = jnp.concatenate(tiles, axis=0).astype(jnp.bfloat16)

    @pl.loop(0, 4 * (PAIRS - 1))
    def _(step):
        pick(step, False)

    @pl.loop(0, 4)
    def _(step):
        pick(step, True)

    total = jnp.dot(lhs[...], wall[...], preferred_element_type=jnp.float32)
    out_ref[...] = total.T


def add_kernel(got_ref, out_ref):
    for half in range(2):
        total = got_ref[half]
        for p in range(1, 4):
            total = total + got_ref[2 * p + half]
        out_ref[:, HALF * half:HALF * (half + 1)] = total.astype(jnp.bfloat16)


def local(features, weights, send_rows, gather_map):
    width = features.shape[1]
    par = lax.axis_index("chan") % 2
    flip = [(i, i ^ 1) for i in range(8)]
    duo = [[2 * i, 2 * i + 1] for i in range(4)]
    w0 = weights.reshape(OFFS * width, 256)
    both = lax.all_gather(features.T, "chan", axis=0, tiled=True, axis_index_groups=duo)
    rows = send_rows[0]
    own = jnp.concatenate([both, digits([rows[3], rows[3], rows[4]])], axis=0)
    to_up = jnp.concatenate([both, digits([rows[5], rows[6], rows[7]])], axis=0)
    to_dn = jnp.concatenate([both, digits([rows[0], rows[1], rows[2]])], axis=0)
    up = shift(to_up, 1, 0)
    dn = shift(to_dn, -1, 0)
    w1 = lax.ppermute(w0, "chan", flip)
    strip = jnp.concatenate([own, up, dn], axis=0)
    xp = shift(strip, 0, 1)
    xm = shift(strip, 0, -1)
    vmem = pl.BlockSpec(memory_space=pltpu.VMEM)
    part = pl.pallas_call(
        conv_kernel,
        out_shape=jax.ShapeDtypeStruct((256, HALF), jnp.float32),
        in_specs=[pl.BlockSpec(memory_space=pltpu.SMEM)] + [vmem] * 8,
        out_specs=vmem,
        scratch_shapes=[
            pltpu.VMEM((ROWS, 128), jnp.float32),
            pltpu.VMEM((48, 128), jnp.int32),
            pltpu.VMEM((128, 128), jnp.int32),
            pltpu.SMEM((128, 128), jnp.int32),
            pltpu.VMEM((HALF, 128 * PAIRS), jnp.bfloat16),
            pltpu.VMEM((128 * PAIRS, 256), jnp.bfloat16),
            pltpu.SemaphoreType.DMA,
        ],
        compiler_params=pltpu.CompilerParams(vmem_limit_bytes=40 * 2**20),
        name="conv",
    )(par.reshape(1).astype(jnp.int32), gather_map, own, up, dn, xp, xm, w0, w1)
    got = lax.all_to_all(part, "chan", 0, 0, tiled=True).reshape(8, 32, HALF)
    return pl.pallas_call(
        add_kernel,
        out_shape=jax.ShapeDtypeStruct((32, V), jnp.bfloat16),
        in_specs=[vmem],
        out_specs=vmem,
        name="add",
    )(got).T


def solution(mesh):
    in_specs = (P("space", "chan"), P(None, "chan", None), P("space", None, None), P(None, "space"))
    out_specs = P("space", "chan")
    return jax.shard_map(local, mesh=mesh, in_specs=in_specs, out_specs=out_specs, check_vma=False)
```

```python
import jax
import jax.numpy as jnp
from jax import lax
from jax.experimental import pallas as pl
from jax.experimental.pallas import tpu as pltpu
from jax.sharding import PartitionSpec as P

GRID = 8
V = 1024
HALF = V // 2
HALO = 768
OFFS = 27
CENTRE = 13
PAIRS = 14
MSG = 80
ZERO = 9 * V
ROWS = ZERO + 8
STEPS = ((-1, -1), (-1, 0), (-1, 1), (0, -1), (0, 1), (1, -1), (1, 0), (1, 1))


def shift(value, step_row):
    pairs = [
        (row * GRID + col, (row + step_row) * GRID + col)
        for row in range(GRID)
        for col in range(GRID)
        if 0 <= row + step_row < GRID
    ]
    return lax.ppermute(value, "space", pairs)


def conv_kernel(where_ref, gm_ref, both_ref, outer_ref, w0_ref, w1_ref,
                out_ref, table, digit, lut, comp, index, lhs, wall, sem):
    par = where_ref[0]
    core = where_ref[1]
    sources = [both_ref.at[pl.ds(MSG * i, MSG)] for i in range(6)]
    sources += [outer_ref.at[pl.ds(MSG * i, MSG)] for i in range(3)]
    own_base = 3 * core

    for block, source in enumerate(sources):
        digit[16 * block:16 * block + 16, :] = source[64:80, :HALO].astype(jnp.float32)
    base_of = {
        0: own_base,
        1: jnp.where(core == 0, 6, 0),
        -1: jnp.where(core == 0, 3, 6),
    }
    for number, (step_row, step_col) in enumerate(STEPS):
        block = base_of[step_col] + (0, 1, 2)[step_row]
        high = digit[pl.ds(16 * block + number, 1), :]
        low = digit[pl.ds(16 * block + 8 + number, 1), :]
        slot = (high * 32.0 + low).astype(jnp.int32)
        slot = jnp.where(slot >= V, ZERO, slot + block * V)
        for j in range(HALO // 128):
            lut[6 * number + j:6 * number + j + 1, :] = slot[:, 128 * j:128 * (j + 1)]

    def compose(c):
        for k0 in range(0, 32, 8):
            rows = min(8, OFFS - k0)
            here = gm_ref[k0:k0 + rows, pl.ds(pl.multiple_of(par * HALF + 128 * c, 128), 128)]
            if rows < 8:
                here = jnp.concatenate([here, jnp.full((8 - rows, 128), 8 * HALO + V, jnp.int32)], axis=0)
            slot = here - V
            hi = lax.shift_right_arithmetic(slot, 7)
            lo = slot & 127
            got = jnp.where(slot < 0, here + own_base * V, ZERO)
            for t in range(8 * HALO // 128):
                line = jnp.broadcast_to(lut[t:t + 1, :], (8, 128))
                value = jnp.take_along_axis(line, lo, axis=1)
                got = jnp.where(hi == t, value, got)
            comp[32 * c + k0:32 * c + k0 + 8, :] = got
            if rows < 8:
                comp[32 * c + CENTRE:32 * c + CENTRE + 1, :] = got[rows - 1:rows, :]
        rows = pl.ds(32 * c, 32)
        copy = pltpu.make_async_copy(comp.at[rows], index.at[rows], sem.at[c])
        copy.start()
        return copy

    copies = [compose(c) for c in range(HALF // 128)]

    for block, source in enumerate(sources):
        for c in range(V // 128):
            x = source[0:64, 128 * c:128 * (c + 1)].astype(jnp.float32)
            x = jnp.concatenate([x, x], axis=0)
            table[block * V + 128 * c:block * V + 128 * (c + 1), :] = x.T
    table[ZERO:ROWS, :] = jnp.zeros((8, 128), jnp.float32)

    for place in range(OFFS):
        k = {CENTRE: OFFS - 1, OFFS - 1: CENTRE}.get(place, place)
        for side, w_ref in ((par, w0_ref), (1 - par, w1_ref)):
            wall[pl.ds(pl.multiple_of(64 * place + 32 * side, 32), 32), :] = w_ref[32 * k:32 * k + 32, :]
    wall[64 * OFFS:, :] = jnp.zeros((64, 256), jnp.bfloat16)

    own = pl.multiple_of(own_base * V + par * HALF, 128)
    lhs[:, 128 * (PAIRS - 1):] = table[pl.ds(own, HALF), :].astype(jnp.bfloat16)

    sub = lax.broadcasted_iota(jnp.int32, (8, 128), 0)
    lane = lax.broadcasted_iota(jnp.int32, (8, 128), 1)
    masks = [sub == j for j in range(8)]
    left = lane < 64
    for copy in copies:
        copy.wait()

    @pl.loop(0, 4 * (PAIRS - 1))
    def _(step):
        pair = step >> 2
        quarter = step & 3
        line = quarter * 32 + 2 * pair
        for h in range(0, 128, 16):
            tiles = []
            for g in range(h, h + 16, 8):
                sides = []
                for side in range(2):
                    acc = None
                    for j in range(8):
                        at = index.at[pl.ds(side, 127), pl.ds(g + j, 1)][line, 0]
                        row = table[pl.ds(at, 8, stride=0), :]
                        acc = row if acc is None else jnp.where(masks[j], row, acc)
                    sides.append(acc)
                tiles.append(jnp.where(left, sides[0], sides[1]))
            rows = pl.ds(pl.multiple_of(quarter * 128 + h, 16), 16)
            lanes = pl.ds(pl.multiple_of(128 * pair, 128), 128)
            lhs[rows, lanes] = jnp.concatenate(tiles, axis=0).astype(jnp.bfloat16)

    total = jnp.dot(lhs[...], wall[...], preferred_element_type=jnp.float32)
    out_ref[...] = total.T


def add_kernel(got_ref, out_ref):
    for half in range(2):
        total = got_ref[half]
        for p in range(1, 4):
            total = total + got_ref[2 * p + half]
        out_ref[:, HALF * half:HALF * (half + 1)] = total.astype(jnp.bfloat16)


def local(features, weights, send_rows, gather_map):
    width = features.shape[1]
    par = lax.axis_index("chan") % 2
    core = lax.axis_index("space") % 2
    flip = [(i, i ^ 1) for i in range(8)]
    duo = [[2 * i, 2 * i + 1] for i in range(4)]
    chips = [[2 * i, 2 * i + 1] for i in range(GRID * GRID // 2)]
    facing = [
        (row * GRID + a, row * GRID + b)
        for row in range(GRID)
        for col in range(1, GRID - 1, 2)
        for a, b in ((col, col + 1), (col + 1, col))
    ]
    w0 = weights.reshape(OFFS * width, 256)
    mine = lax.all_gather(features.T, "chan", axis=0, tiled=True, axis_index_groups=duo)
    rows = jnp.pad(send_rows[0], ((0, 0), (0, V - HALO)))
    message = jnp.concatenate([mine, (rows >> 5).astype(jnp.bfloat16), (rows & 31).astype(jnp.bfloat16)], axis=0)
    up = shift(message, 1)
    dn = shift(message, -1)
    w1 = lax.ppermute(w0, "chan", flip)
    strip = jnp.concatenate([message, up, dn], axis=0)
    outer = lax.ppermute(strip, "space", facing)
    both = lax.all_gather(strip, "space", axis=0, tiled=True, axis_index_groups=chips)
    vmem = pl.BlockSpec(memory_space=pltpu.VMEM)
    part = pl.pallas_call(
        conv_kernel,
        out_shape=jax.ShapeDtypeStruct((256, HALF), jnp.float32),
        in_specs=[pl.BlockSpec(memory_space=pltpu.SMEM)] + [vmem] * 5,
        out_specs=vmem,
        scratch_shapes=[
            pltpu.VMEM((ROWS, 128), jnp.float32),
            pltpu.VMEM((144, HALO), jnp.float32),
            pltpu.VMEM((48, 128), jnp.int32),
            pltpu.VMEM((128, 128), jnp.int32),
            pltpu.SMEM((128, 128), jnp.int32),
            pltpu.VMEM((HALF, 128 * PAIRS), jnp.bfloat16),
            pltpu.VMEM((128 * PAIRS, 256), jnp.bfloat16),
            pltpu.SemaphoreType.DMA((4,)),
        ],
        compiler_params=pltpu.CompilerParams(vmem_limit_bytes=40 * 2**20),
        name="conv",
    )(jnp.stack([par, core]).astype(jnp.int32), gather_map, both, outer, w0, w1)
    got = lax.all_to_all(part, "chan", 0, 0, tiled=True).reshape(8, 32, HALF)
    return pl.pallas_call(
        add_kernel,
        out_shape=jax.ShapeDtypeStruct((32, V), jnp.bfloat16),
        in_specs=[vmem],
        out_specs=vmem,
        compiler_params=pltpu.CompilerParams(vmem_limit_bytes=4 * 2**20),
        name="add",
    )(got).T


def solution(mesh):
    in_specs = (P("space", "chan"), P(None, "chan", None), P("space", None, None), P(None, "space"))
    out_specs = P("space", "chan")
    return jax.shard_map(local, mesh=mesh, in_specs=in_specs, out_specs=out_specs, check_vma=False)
```

```python
import jax
import jax.numpy as jnp
from jax import lax
from jax.experimental import pallas as pl
from jax.experimental.pallas import tpu as pltpu
from jax.sharding import PartitionSpec as P

GRID = 8
V = 1024
HALF = V // 2
HALO = 768
OFFS = 27
CENTRE = 13
PAIRS = 14
MSG = 80
ZERO = 9 * V
ROWS = ZERO + 8
STEPS = ((-1, -1), (-1, 0), (-1, 1), (0, -1), (0, 1), (1, -1), (1, 0), (1, 1))


def shift(value, step_row):
    pairs = [
        (row * GRID + col, (row + step_row) * GRID + col)
        for row in range(GRID)
        for col in range(GRID)
        if 0 <= row + step_row < GRID
    ]
    return lax.ppermute(value, "space", pairs)


def conv_kernel(where_ref, gm_ref, both_ref, outer_ref, w0_ref, w1_ref,
                out_ref, table, digit, lut, comp, index, lhs, wall, sem):
    par = where_ref[0]
    core = where_ref[1]
    sources = [both_ref.at[pl.ds(MSG * i, MSG)] for i in range(6)]
    sources += [outer_ref.at[pl.ds(MSG * i, MSG)] for i in range(3)]
    own_base = 3 * core

    for block, source in enumerate(sources):
        digit[16 * block:16 * block + 16, :] = source[64:80, :HALO].astype(jnp.float32)
    base_of = {
        0: own_base,
        1: jnp.where(core == 0, 6, 0),
        -1: jnp.where(core == 0, 3, 6),
    }
    for number, (step_row, step_col) in enumerate(STEPS):
        block = base_of[step_col] + (0, 1, 2)[step_row]
        high = digit[pl.ds(16 * block + number, 1), :]
        low = digit[pl.ds(16 * block + 8 + number, 1), :]
        slot = (high * 32.0 + low).astype(jnp.int32)
        slot = jnp.where(slot >= V, ZERO, slot + block * V)
        for j in range(HALO // 128):
            lut[6 * number + j:6 * number + j + 1, :] = slot[:, 128 * j:128 * (j + 1)]

    def compose(c):
        for k0 in range(0, 32, 8):
            rows = min(8, OFFS - k0)
            here = gm_ref[k0:k0 + rows, pl.ds(pl.multiple_of(par * HALF + 128 * c, 128), 128)]
            if rows < 8:
                here = jnp.concatenate([here, jnp.full((8 - rows, 128), 8 * HALO + V, jnp.int32)], axis=0)
            slot = here - V
            hi = lax.shift_right_arithmetic(slot, 7)
            lo = slot & 127
            got = jnp.where(slot < 0, here + own_base * V, ZERO)
            for t in range(8 * HALO // 128):
                line = jnp.broadcast_to(lut[t:t + 1, :], (8, 128))
                value = jnp.take_along_axis(line, lo, axis=1)
                got = jnp.where(hi == t, value, got)
            comp[32 * c + k0:32 * c + k0 + 8, :] = got
            if rows < 8:
                comp[32 * c + CENTRE:32 * c + CENTRE + 1, :] = got[rows - 1:rows, :]
        rows = pl.ds(32 * c, 32)
        copy = pltpu.make_async_copy(comp.at[rows], index.at[rows], sem.at[c])
        copy.start()
        return copy

    copies = [compose(c) for c in range(HALF // 128)]

    for block, source in enumerate(sources):
        for c in range(V // 128):
            x = source[0:64, 128 * c:128 * (c + 1)].astype(jnp.float32)
            x = jnp.concatenate([x, x], axis=0)
            table[block * V + 128 * c:block * V + 128 * (c + 1), :] = x.T
    table[ZERO:ROWS, :] = jnp.zeros((8, 128), jnp.float32)

    for place in range(OFFS):
        k = {CENTRE: OFFS - 1, OFFS - 1: CENTRE}.get(place, place)
        k1 = k if k <= CENTRE else k + 1
        for side, w_ref, at in ((par, w0_ref, 32 * k), (1 - par, w1_ref, 32 * k1)):
            wall[pl.ds(pl.multiple_of(64 * place + 32 * side, 32), 32), :] = w_ref[at:at + 32, :]
    wall[64 * OFFS:, :] = jnp.zeros((64, 256), jnp.bfloat16)

    own = pl.multiple_of(own_base * V + par * HALF, 128)
    lhs[:, 128 * (PAIRS - 1):] = table[pl.ds(own, HALF), :].astype(jnp.bfloat16)

    sub = lax.broadcasted_iota(jnp.int32, (8, 128), 0)
    lane = lax.broadcasted_iota(jnp.int32, (8, 128), 1)
    masks = [sub == j for j in range(8)]
    left = lane < 64
    for copy in copies:
        copy.wait()

    @pl.loop(0, 4 * (PAIRS - 1))
    def _(step):
        pair = step >> 2
        quarter = step & 3
        line = quarter * 32 + 2 * pair
        for h in range(0, 128, 16):
            tiles = []
            for g in range(h, h + 16, 8):
                sides = []
                for side in range(2):
                    acc = None
                    for j in range(8):
                        at = index.at[pl.ds(side, 127), pl.ds(g + j, 1)][line, 0]
                        row = table[pl.ds(at, 8, stride=0), :]
                        acc = row if acc is None else jnp.where(masks[j], row, acc)
                    sides.append(acc)
                tiles.append(jnp.where(left, sides[0], sides[1]))
            rows = pl.ds(pl.multiple_of(quarter * 128 + h, 16), 16)
            lanes = pl.ds(pl.multiple_of(128 * pair, 128), 128)
            lhs[rows, lanes] = jnp.concatenate(tiles, axis=0).astype(jnp.bfloat16)

    total = jnp.dot(lhs[...], wall[...], preferred_element_type=jnp.float32)
    out_ref[...] = total.T


def add_kernel(got_ref, out_ref):
    for half in range(2):
        total = got_ref[half]
        for p in range(1, 4):
            total = total + got_ref[2 * p + half]
        out_ref[:, HALF * half:HALF * (half + 1)] = total.astype(jnp.bfloat16)


def local(features, weights, send_rows, gather_map):
    width = features.shape[1]
    par = lax.axis_index("chan") % 2
    core = lax.axis_index("space") % 2
    flip = [(i, i ^ 1) for i in range(8)]
    duo = [[2 * i, 2 * i + 1] for i in range(4)]
    chips = [[2 * i, 2 * i + 1] for i in range(GRID * GRID // 2)]
    facing = [
        (row * GRID + a, row * GRID + b)
        for row in range(GRID)
        for col in range(1, GRID - 1, 2)
        for a, b in ((col, col + 1), (col + 1, col))
    ]
    w0 = weights.reshape(OFFS * width, 256)
    mine = lax.all_gather(features.T, "chan", axis=0, tiled=True, axis_index_groups=duo)
    rows = jnp.pad(send_rows[0], ((0, 0), (0, V - HALO)))
    message = jnp.concatenate([mine, (rows >> 5).astype(jnp.bfloat16), (rows & 31).astype(jnp.bfloat16)], axis=0)
    up = shift(message, 1)
    dn = shift(message, -1)
    part = lax.dynamic_slice_in_dim(w0, core * (CENTRE * width), (CENTRE + 1) * width, 0)
    part = lax.ppermute(part, "chan", flip)
    strip = jnp.concatenate([message, up, dn], axis=0)
    strip, part = lax.optimization_barrier((strip, part))
    outer = lax.ppermute(strip, "space", facing)
    both = lax.all_gather(strip, "space", axis=0, tiled=True, axis_index_groups=chips)
    w1 = lax.all_gather(part, "space", axis=0, tiled=True, axis_index_groups=chips)
    vmem = pl.BlockSpec(memory_space=pltpu.VMEM)
    part = pl.pallas_call(
        conv_kernel,
        out_shape=jax.ShapeDtypeStruct((256, HALF), jnp.float32),
        in_specs=[pl.BlockSpec(memory_space=pltpu.SMEM)] + [vmem] * 5,
        out_specs=vmem,
        scratch_shapes=[
            pltpu.VMEM((ROWS, 128), jnp.float32),
            pltpu.VMEM((144, HALO), jnp.float32),
            pltpu.VMEM((48, 128), jnp.int32),
            pltpu.VMEM((128, 128), jnp.int32),
            pltpu.SMEM((128, 128), jnp.int32),
            pltpu.VMEM((HALF, 128 * PAIRS), jnp.bfloat16),
            pltpu.VMEM((128 * PAIRS, 256), jnp.bfloat16),
            pltpu.SemaphoreType.DMA((4,)),
        ],
        compiler_params=pltpu.CompilerParams(vmem_limit_bytes=40 * 2**20),
        name="conv",
    )(jnp.stack([par, core]).astype(jnp.int32), gather_map, both, outer, w0, w1)
    got = lax.all_to_all(part, "chan", 0, 0, tiled=True).reshape(8, 32, HALF)
    return pl.pallas_call(
        add_kernel,
        out_shape=jax.ShapeDtypeStruct((32, V), jnp.bfloat16),
        in_specs=[vmem],
        out_specs=vmem,
        compiler_params=pltpu.CompilerParams(vmem_limit_bytes=4 * 2**20),
        name="add",
    )(got).T


def solution(mesh):
    in_specs = (P("space", "chan"), P(None, "chan", None), P("space", None, None), P(None, "space"))
    out_specs = P("space", "chan")
    return jax.shard_map(local, mesh=mesh, in_specs=in_specs, out_specs=out_specs, check_vma=False)
```

```python
import jax
import jax.numpy as jnp
from jax import lax
from jax.experimental import pallas as pl
from jax.experimental.pallas import tpu as pltpu
from jax.sharding import PartitionSpec as P

GRID = 8
V = 1024
HALF = V // 2
HALO = 768
OFFS = 27
CENTRE = 13
PAIRS = 14
MSG = 80
ZERO = 9 * V
ROWS = ZERO + 8
STEPS = ((-1, -1), (-1, 0), (-1, 1), (0, -1), (0, 1), (1, -1), (1, 0), (1, 1))


def shift(value, step_row):
    pairs = [
        (row * GRID + col, (row + step_row) * GRID + col)
        for row in range(GRID)
        for col in range(GRID)
        if 0 <= row + step_row < GRID
    ]
    return lax.ppermute(value, "space", pairs)


def conv_kernel(where_ref, gm_ref, both_ref, outer_ref, w0_ref, w1_ref,
                out_ref, table, digit, lut, comp, index, lhs, wall, sem):
    par = where_ref[0]
    core = where_ref[1]
    sources = [both_ref.at[pl.ds(MSG * i, MSG)] for i in range(6)]
    sources += [outer_ref.at[pl.ds(MSG * i, MSG)] for i in range(3)]
    own_base = 3 * core

    for block, source in enumerate(sources):
        digit[16 * block:16 * block + 16, :] = source[64:80, :HALO].astype(jnp.float32)
    base_of = {
        0: own_base,
        1: jnp.where(core == 0, 6, 0),
        -1: jnp.where(core == 0, 3, 6),
    }
    for number, (step_row, step_col) in enumerate(STEPS):
        block = base_of[step_col] + (0, 1, 2)[step_row]
        high = digit[pl.ds(16 * block + number, 1), :]
        low = digit[pl.ds(16 * block + 8 + number, 1), :]
        slot = (high * 32.0 + low).astype(jnp.int32)
        slot = jnp.where(slot >= V, ZERO, slot + block * V)
        for j in range(HALO // 128):
            lut[6 * number + j:6 * number + j + 1, :] = slot[:, 128 * j:128 * (j + 1)]

    def compose(c):
        for k0 in range(0, 32, 8):
            rows = min(8, OFFS - k0)
            here = gm_ref[k0:k0 + rows, pl.ds(pl.multiple_of(par * HALF + 128 * c, 128), 128)]
            if rows < 8:
                here = jnp.concatenate([here, jnp.full((8 - rows, 128), 8 * HALO + V, jnp.int32)], axis=0)
            slot = here - V
            hi = lax.shift_right_arithmetic(slot, 7)
            lo = slot & 127
            got = jnp.where(slot < 0, here + own_base * V, ZERO)
            for t in range(8 * HALO // 128):
                line = jnp.broadcast_to(lut[t:t + 1, :], (8, 128))
                value = jnp.take_along_axis(line, lo, axis=1)
                got = jnp.where(hi == t, value, got)
            comp[32 * c + k0:32 * c + k0 + 8, :] = got
            if rows < 8:
                comp[32 * c + CENTRE:32 * c + CENTRE + 1, :] = got[rows - 1:rows, :]
        rows = pl.ds(32 * c, 32)
        copy = pltpu.make_async_copy(comp.at[rows], index.at[rows], sem.at[c])
        copy.start()
        return copy

    copies = [compose(c) for c in range(HALF // 128)]

    for block, source in enumerate(sources):
        for c in range(V // 128):
            x = source[0:64, 128 * c:128 * (c + 1)].astype(jnp.float32)
            x = jnp.concatenate([x, x], axis=0)
            table[block * V + 128 * c:block * V + 128 * (c + 1), :] = x.T
    table[ZERO:ROWS, :] = jnp.zeros((8, 128), jnp.float32)

    for place in range(OFFS):
        k = {CENTRE: OFFS - 1, OFFS - 1: CENTRE}.get(place, place)
        k1 = k if k <= CENTRE else k + 1
        for side, w_ref, at in ((par, w0_ref, 32 * k), (1 - par, w1_ref, 32 * k1)):
            wall[pl.ds(pl.multiple_of(64 * place + 32 * side, 32), 32), :] = w_ref[at:at + 32, :]
    wall[64 * OFFS:, :] = jnp.zeros((64, 256), jnp.bfloat16)

    own = pl.multiple_of(own_base * V + par * HALF, 128)
    lhs[:, 128 * (PAIRS - 1):] = table[pl.ds(own, HALF), :].astype(jnp.bfloat16)

    sub = lax.broadcasted_iota(jnp.int32, (8, 128), 0)
    lane = lax.broadcasted_iota(jnp.int32, (8, 128), 1)
    masks = [sub == j for j in range(8)]
    left = lane < 64
    for copy in copies:
        copy.wait()

    @pl.loop(0, 4 * (PAIRS - 1))
    def _(step):
        pair = step >> 2
        quarter = step & 3
        line = quarter * 32 + 2 * pair
        for h in range(0, 128, 16):
            tiles = []
            for g in range(h, h + 16, 8):
                sides = []
                for side in range(2):
                    acc = None
                    for j in range(8):
                        at = index.at[pl.ds(side, 127), pl.ds(g + j, 1)][line, 0]
                        row = table[pl.ds(at, 8, stride=0), :]
                        acc = row if acc is None else jnp.where(masks[j], row, acc)
                    sides.append(acc)
                tiles.append(jnp.where(left, sides[0], sides[1]))
            rows = pl.ds(pl.multiple_of(quarter * 128 + h, 16), 16)
            lanes = pl.ds(pl.multiple_of(128 * pair, 128), 128)
            lhs[rows, lanes] = jnp.concatenate(tiles, axis=0).astype(jnp.bfloat16)

    total = jnp.dot(lhs[...], wall[...], preferred_element_type=jnp.float32)
    out_ref[...] = total.T


def add_kernel(got_ref, out_ref):
    for half in range(2):
        total = got_ref[half]
        for p in range(1, 4):
            total = total + got_ref[2 * p + half]
        out_ref[:, HALF * half:HALF * (half + 1)] = total.astype(jnp.bfloat16)


def local(features, weights, send_rows, gather_map):
    width = features.shape[1]
    par = lax.axis_index("chan") % 2
    core = lax.axis_index("space") % 2
    flip = [(i, i ^ 1) for i in range(8)]
    duo = [[2 * i, 2 * i + 1] for i in range(4)]
    chips = [[2 * i, 2 * i + 1] for i in range(GRID * GRID // 2)]
    facing = [
        (row * GRID + a, row * GRID + b)
        for row in range(GRID)
        for col in range(1, GRID - 1, 2)
        for a, b in ((col, col + 1), (col + 1, col))
    ]
    w0 = weights.reshape(OFFS * width, 256)
    part = lax.dynamic_slice_in_dim(w0, core * (CENTRE * width), (CENTRE + 1) * width, 0)
    part = lax.ppermute(part, "chan", flip)
    mine = lax.all_gather(features.T, "chan", axis=0, tiled=True, axis_index_groups=duo)
    rows = jnp.pad(send_rows[0], ((0, 0), (0, V - HALO)))
    message = jnp.concatenate([mine, (rows >> 5).astype(jnp.bfloat16), (rows & 31).astype(jnp.bfloat16)], axis=0)
    message, part = lax.optimization_barrier((message, part))
    up = shift(message, 1)
    dn = shift(message, -1)
    strip = jnp.concatenate([message, up, dn], axis=0)
    w1 = lax.all_gather(part, "space", axis=0, tiled=True, axis_index_groups=chips)
    strip, w1 = lax.optimization_barrier((strip, w1))
    outer = lax.ppermute(strip, "space", facing)
    both = lax.all_gather(strip, "space", axis=0, tiled=True, axis_index_groups=chips)
    vmem = pl.BlockSpec(memory_space=pltpu.VMEM)
    part = pl.pallas_call(
        conv_kernel,
        out_shape=jax.ShapeDtypeStruct((256, HALF), jnp.float32),
        in_specs=[pl.BlockSpec(memory_space=pltpu.SMEM)] + [vmem] * 5,
        out_specs=vmem,
        scratch_shapes=[
            pltpu.VMEM((ROWS, 128), jnp.float32),
            pltpu.VMEM((144, HALO), jnp.float32),
            pltpu.VMEM((48, 128), jnp.int32),
            pltpu.VMEM((128, 128), jnp.int32),
            pltpu.SMEM((128, 128), jnp.int32),
            pltpu.VMEM((HALF, 128 * PAIRS), jnp.bfloat16),
            pltpu.VMEM((128 * PAIRS, 256), jnp.bfloat16),
            pltpu.SemaphoreType.DMA((4,)),
        ],
        compiler_params=pltpu.CompilerParams(vmem_limit_bytes=40 * 2**20),
        name="conv",
    )(jnp.stack([par, core]).astype(jnp.int32), gather_map, both, outer, w0, w1)
    got = lax.all_to_all(part, "chan", 0, 0, tiled=True).reshape(8, 32, HALF)
    return pl.pallas_call(
        add_kernel,
        out_shape=jax.ShapeDtypeStruct((32, V), jnp.bfloat16),
        in_specs=[vmem],
        out_specs=vmem,
        compiler_params=pltpu.CompilerParams(vmem_limit_bytes=4 * 2**20),
        name="add",
    )(got).T


def solution(mesh):
    in_specs = (P("space", "chan"), P(None, "chan", None), P("space", None, None), P(None, "space"))
    out_specs = P("space", "chan")
    return jax.shard_map(local, mesh=mesh, in_specs=in_specs, out_specs=out_specs, check_vma=False)
```

```python
import jax
import jax.numpy as jnp
from jax import lax
from jax.experimental import pallas as pl
from jax.experimental.pallas import tpu as pltpu
from jax.sharding import PartitionSpec as P

GRID = 8
V = 1024
HALF = V // 2
HALO = 768
OFFS = 27
CENTRE = 13
PAIRS = 14
MSG = 72
ZERO = 9 * V
ROWS = ZERO + 8
FIRST = (3, 5, 0)
STEPS = ((-1, -1), (-1, 0), (-1, 1), (0, -1), (0, 1), (1, -1), (1, 0), (1, 1))


def shift(value, step_row, step_col):
    pairs = [
        (row * GRID + col, (row + step_row) * GRID + col + step_col)
        for row in range(GRID)
        for col in range(GRID)
        if 0 <= row + step_row < GRID and 0 <= col + step_col < GRID
    ]
    return lax.ppermute(value, "space", pairs)


def conv_kernel(par_ref, gm_ref, own_ref, up_ref, dn_ref, left_ref, right_ref, w0_ref, w1_ref,
                out_ref, table, digit, lut, comp, index, lhs, wall, sem):
    par = par_ref[0]
    sources = [own_ref, up_ref, dn_ref]
    sources += [ref.at[pl.ds(MSG * i, MSG)] for ref in (left_ref, right_ref) for i in range(3)]

    for block, source in enumerate(sources):
        digit[8 * block:8 * block + 8, :] = source[64:72, :HALO].astype(jnp.float32)
    for number, (step_row, step_col) in enumerate(STEPS):
        sent = (0, 1, 2)[step_row]
        block = 3 * (0, 1, 2)[step_col] + sent
        at = 8 * block + number - FIRST[sent]
        high = digit[at:at + 1, :]
        low = digit[at + 3:at + 4, :]
        slot = (high * 32.0 + low).astype(jnp.int32)
        slot = jnp.where(slot >= V, ZERO, slot + block * V)
        for j in range(HALO // 128):
            lut[6 * number + j:6 * number + j + 1, :] = slot[:, 128 * j:128 * (j + 1)]

    def compose(c):
        for k0 in range(0, 32, 8):
            rows = min(8, OFFS - k0)
            here = gm_ref[k0:k0 + rows, pl.ds(pl.multiple_of(par * HALF + 128 * c, 128), 128)]
            if rows < 8:
                here = jnp.concatenate([here, jnp.full((8 - rows, 128), 8 * HALO + V, jnp.int32)], axis=0)
            slot = here - V
            hi = lax.shift_right_arithmetic(slot, 7)
            lo = slot & 127
            got = jnp.where(slot < 0, here, ZERO)
            for t in range(8 * HALO // 128):
                line = jnp.broadcast_to(lut[t:t + 1, :], (8, 128))
                value = jnp.take_along_axis(line, lo, axis=1)
                got = jnp.where(hi == t, value, got)
            comp[32 * c + k0:32 * c + k0 + 8, :] = got
            if rows < 8:
                comp[32 * c + CENTRE:32 * c + CENTRE + 1, :] = got[rows - 1:rows, :]
        rows = pl.ds(32 * c, 32)
        copy = pltpu.make_async_copy(comp.at[rows], index.at[rows], sem.at[c])
        copy.start()
        return copy

    copies = [compose(c) for c in range(HALF // 128)]

    for block, source in enumerate(sources):
        for c in range(V // 128):
            x = source[0:64, 128 * c:128 * (c + 1)].astype(jnp.float32)
            x = jnp.concatenate([x, x], axis=0)
            table[block * V + 128 * c:block * V + 128 * (c + 1), :] = x.T
    table[ZERO:ROWS, :] = jnp.zeros((8, 128), jnp.float32)

    for place in range(OFFS):
        k = {CENTRE: OFFS - 1, OFFS - 1: CENTRE}.get(place, place)
        for side, w_ref in ((par, w0_ref), (1 - par, w1_ref)):
            wall[pl.ds(pl.multiple_of(64 * place + 32 * side, 32), 32), :] = w_ref[32 * k:32 * k + 32, :]
    wall[64 * OFFS:, :] = jnp.zeros((64, 256), jnp.bfloat16)

    own = pl.multiple_of(par * HALF, 128)
    lhs[:, 128 * (PAIRS - 1):] = table[pl.ds(own, HALF), :].astype(jnp.bfloat16)

    sub = lax.broadcasted_iota(jnp.int32, (8, 128), 0)
    lane = lax.broadcasted_iota(jnp.int32, (8, 128), 1)
    masks = [sub == j for j in range(8)]
    left = lane < 64
    for copy in copies:
        copy.wait()

    @pl.loop(0, 4 * (PAIRS - 1))
    def _(step):
        pair = step >> 2
        quarter = step & 3
        line = quarter * 32 + 2 * pair
        for h in range(0, 128, 16):
            tiles = []
            for g in range(h, h + 16, 8):
                sides = []
                for side in range(2):
                    acc = None
                    for j in range(8):
                        at = index.at[pl.ds(side, 127), pl.ds(g + j, 1)][line, 0]
                        row = table[pl.ds(at, 8, stride=0), :]
                        acc = row if acc is None else jnp.where(masks[j], row, acc)
                    sides.append(acc)
                tiles.append(jnp.where(left, sides[0], sides[1]))
            rows = pl.ds(pl.multiple_of(quarter * 128 + h, 16), 16)
            lanes = pl.ds(pl.multiple_of(128 * pair, 128), 128)
            lhs[rows, lanes] = jnp.concatenate(tiles, axis=0).astype(jnp.bfloat16)

    total = jnp.dot(lhs[...], wall[...], preferred_element_type=jnp.float32)
    out_ref[...] = total.T


def add_kernel(got_ref, out_ref):
    for half in range(2):
        total = got_ref[half]
        for p in range(1, 4):
            total = total + got_ref[2 * p + half]
        out_ref[:, HALF * half:HALF * (half + 1)] = total.astype(jnp.bfloat16)


def local(features, weights, send_rows, gather_map):
    width = features.shape[1]
    par = lax.axis_index("chan") % 2
    flip = [(i, i ^ 1) for i in range(8)]
    duo = [[2 * i, 2 * i + 1] for i in range(4)]
    w0 = weights.reshape(OFFS * width, 256)
    mine = lax.all_gather(features.T, "chan", axis=0, tiled=True, axis_index_groups=duo)
    rows = jnp.pad(send_rows[0], ((0, 0), (0, V - HALO)))
    high, low = (rows >> 5).astype(jnp.bfloat16), (rows & 31).astype(jnp.bfloat16)
    blank = jnp.zeros((2, V), jnp.bfloat16)

    def message(first):
        return jnp.concatenate([mine, high[first:first + 3], low[first:first + 3], blank], axis=0)

    own = message(FIRST[0])
    up = shift(message(FIRST[1]), 1, 0)
    dn = shift(message(FIRST[2]), -1, 0)
    w1 = lax.ppermute(w0, "chan", flip)
    strip = jnp.concatenate([own, up, dn], axis=0)
    left = shift(strip, 0, 1)
    right = shift(strip, 0, -1)
    vmem = pl.BlockSpec(memory_space=pltpu.VMEM)
    part = pl.pallas_call(
        conv_kernel,
        out_shape=jax.ShapeDtypeStruct((256, HALF), jnp.float32),
        in_specs=[pl.BlockSpec(memory_space=pltpu.SMEM)] + [vmem] * 8,
        out_specs=vmem,
        scratch_shapes=[
            pltpu.VMEM((ROWS, 128), jnp.float32),
            pltpu.VMEM((72, HALO), jnp.float32),
            pltpu.VMEM((48, 128), jnp.int32),
            pltpu.VMEM((128, 128), jnp.int32),
            pltpu.SMEM((128, 128), jnp.int32),
            pltpu.VMEM((HALF, 128 * PAIRS), jnp.bfloat16),
            pltpu.VMEM((128 * PAIRS, 256), jnp.bfloat16),
            pltpu.SemaphoreType.DMA((4,)),
        ],
        compiler_params=pltpu.CompilerParams(vmem_limit_bytes=40 * 2**20),
        name="conv",
    )(par.reshape(1).astype(jnp.int32), gather_map, own, up, dn, left, right, w0, w1)
    got = lax.all_to_all(part, "chan", 0, 0, tiled=True).reshape(8, 32, HALF)
    return pl.pallas_call(
        add_kernel,
        out_shape=jax.ShapeDtypeStruct((32, V), jnp.bfloat16),
        in_specs=[vmem],
        out_specs=vmem,
        compiler_params=pltpu.CompilerParams(vmem_limit_bytes=4 * 2**20),
        name="add",
    )(got).T


def solution(mesh):
    in_specs = (P("space", "chan"), P(None, "chan", None), P("space", None, None), P(None, "space"))
    out_specs = P("space", "chan")
    return jax.shard_map(local, mesh=mesh, in_specs=in_specs, out_specs=out_specs, check_vma=False)
```

```python
import jax
import jax.numpy as jnp
from jax import lax
from jax.experimental import pallas as pl
from jax.experimental.pallas import tpu as pltpu
from jax.sharding import PartitionSpec as P

GRID = 8
V = 1024
HALF = V // 2
HALO = 768
OFFS = 27
CENTRE = 13
PAIRS = 14
MSG = 72
ZERO = 9 * V
ROWS = ZERO + 8
FIRST = (3, 5, 0)
STEPS = ((-1, -1), (-1, 0), (-1, 1), (0, -1), (0, 1), (1, -1), (1, 0), (1, 1))


def shift(value, step_row, step_col):
    pairs = [
        (row * GRID + col, (row + step_row) * GRID + col + step_col)
        for row in range(GRID)
        for col in range(GRID)
        if 0 <= row + step_row < GRID and 0 <= col + step_col < GRID
    ]
    return lax.ppermute(value, "space", pairs)


def conv_kernel(where_ref, gm_ref, both_ref, outer_ref, w0_ref, w1_ref,
                out_ref, table, digit, lut, comp, index, lhs, wall, sem):
    par = where_ref[0]
    core = where_ref[1]
    sources = [both_ref.at[pl.ds(MSG * i, MSG)] for i in range(6)]
    sources += [outer_ref.at[pl.ds(MSG * i, MSG)] for i in range(3)]
    own_base = 3 * core
    base_of = (own_base, jnp.where(core == 0, 6, 0), jnp.where(core == 0, 3, 6))

    for block, source in enumerate(sources):
        digit[8 * block:8 * block + 8, :] = source[64:72, :HALO].astype(jnp.float32)
    for number, (step_row, step_col) in enumerate(STEPS):
        sent = (0, 1, 2)[step_row]
        block = base_of[step_col] + sent
        at = 8 * block + number - FIRST[sent]
        high = digit[pl.ds(at, 1), :]
        low = digit[pl.ds(at + 3, 1), :]
        slot = (high * 32.0 + low).astype(jnp.int32)
        slot = jnp.where(slot >= V, ZERO, slot + block * V)
        for j in range(HALO // 128):
            lut[6 * number + j:6 * number + j + 1, :] = slot[:, 128 * j:128 * (j + 1)]

    def compose(c):
        for k0 in range(0, 32, 8):
            rows = min(8, OFFS - k0)
            here = gm_ref[k0:k0 + rows, pl.ds(pl.multiple_of(par * HALF + 128 * c, 128), 128)]
            if rows < 8:
                here = jnp.concatenate([here, jnp.full((8 - rows, 128), 8 * HALO + V, jnp.int32)], axis=0)
            slot = here - V
            hi = lax.shift_right_arithmetic(slot, 7)
            lo = slot & 127
            got = jnp.where(slot < 0, here + own_base * V, ZERO)
            for t in range(8 * HALO // 128):
                line = jnp.broadcast_to(lut[t:t + 1, :], (8, 128))
                value = jnp.take_along_axis(line, lo, axis=1)
                got = jnp.where(hi == t, value, got)
            comp[32 * c + k0:32 * c + k0 + 8, :] = got
            if rows < 8:
                comp[32 * c + CENTRE:32 * c + CENTRE + 1, :] = got[rows - 1:rows, :]
        rows = pl.ds(32 * c, 32)
        copy = pltpu.make_async_copy(comp.at[rows], index.at[rows], sem.at[c])
        copy.start()
        return copy

    copies = [compose(c) for c in range(HALF // 128)]

    for block, source in enumerate(sources):
        for c in range(V // 128):
            x = source[0:64, 128 * c:128 * (c + 1)].astype(jnp.float32)
            x = jnp.concatenate([x, x], axis=0)
            table[block * V + 128 * c:block * V + 128 * (c + 1), :] = x.T
    table[ZERO:ROWS, :] = jnp.zeros((8, 128), jnp.float32)

    for place in range(OFFS):
        k = {CENTRE: OFFS - 1, OFFS - 1: CENTRE}.get(place, place)
        for side, w_ref in ((par, w0_ref), (1 - par, w1_ref)):
            wall[pl.ds(pl.multiple_of(64 * place + 32 * side, 32), 32), :] = w_ref[32 * k:32 * k + 32, :]
    wall[64 * OFFS:, :] = jnp.zeros((64, 256), jnp.bfloat16)

    own = pl.multiple_of(own_base * V + par * HALF, 128)
    lhs[:, 128 * (PAIRS - 1):] = table[pl.ds(own, HALF), :].astype(jnp.bfloat16)

    sub = lax.broadcasted_iota(jnp.int32, (8, 128), 0)
    lane = lax.broadcasted_iota(jnp.int32, (8, 128), 1)
    masks = [sub == j for j in range(8)]
    left = lane < 64
    for copy in copies:
        copy.wait()

    @pl.loop(0, 4 * (PAIRS - 1))
    def _(step):
        pair = step >> 2
        quarter = step & 3
        line = quarter * 32 + 2 * pair
        for h in range(0, 128, 16):
            tiles = []
            for g in range(h, h + 16, 8):
                sides = []
                for side in range(2):
                    acc = None
                    for j in range(8):
                        at = index.at[pl.ds(side, 127), pl.ds(g + j, 1)][line, 0]
                        row = table[pl.ds(at, 8, stride=0), :]
                        acc = row if acc is None else jnp.where(masks[j], row, acc)
                    sides.append(acc)
                tiles.append(jnp.where(left, sides[0], sides[1]))
            rows = pl.ds(pl.multiple_of(quarter * 128 + h, 16), 16)
            lanes = pl.ds(pl.multiple_of(128 * pair, 128), 128)
            lhs[rows, lanes] = jnp.concatenate(tiles, axis=0).astype(jnp.bfloat16)

    total = jnp.dot(lhs[...], wall[...], preferred_element_type=jnp.float32)
    out_ref[...] = total.T


def add_kernel(got_ref, out_ref):
    for half in range(2):
        total = got_ref[half]
        for p in range(1, 4):
            total = total + got_ref[2 * p + half]
        out_ref[:, HALF * half:HALF * (half + 1)] = total.astype(jnp.bfloat16)


def local(features, weights, send_rows, gather_map):
    width = features.shape[1]
    par = lax.axis_index("chan") % 2
    core = lax.axis_index("space") % 2
    flip = [(i, i ^ 1) for i in range(8)]
    duo = [[2 * i, 2 * i + 1] for i in range(4)]
    chips = [[2 * i, 2 * i + 1] for i in range(GRID * GRID // 2)]
    facing = [
        (row * GRID + a, row * GRID + b)
        for row in range(GRID)
        for col in range(1, GRID - 1, 2)
        for a, b in ((col, col + 1), (col + 1, col))
    ]
    w0 = weights.reshape(OFFS * width, 256)
    mine = lax.all_gather(features.T, "chan", axis=0, tiled=True, axis_index_groups=duo)
    rows = jnp.pad(send_rows[0], ((0, 0), (0, V - HALO)))
    high, low = (rows >> 5).astype(jnp.bfloat16), (rows & 31).astype(jnp.bfloat16)
    blank = jnp.zeros((2, V), jnp.bfloat16)

    def message(first):
        return jnp.concatenate([mine, high[first:first + 3], low[first:first + 3], blank], axis=0)

    own = message(FIRST[0])
    up = shift(message(FIRST[1]), 1, 0)
    dn = shift(message(FIRST[2]), -1, 0)
    w1 = lax.ppermute(w0, "chan", flip)
    strip = jnp.concatenate([own, up, dn], axis=0)
    outer = lax.ppermute(strip, "space", facing)
    both = lax.all_gather(strip, "space", axis=0, tiled=True, axis_index_groups=chips)
    vmem = pl.BlockSpec(memory_space=pltpu.VMEM)
    part = pl.pallas_call(
        conv_kernel,
        out_shape=jax.ShapeDtypeStruct((256, HALF), jnp.float32),
        in_specs=[pl.BlockSpec(memory_space=pltpu.SMEM)] + [vmem] * 5,
        out_specs=vmem,
        scratch_shapes=[
            pltpu.VMEM((ROWS, 128), jnp.float32),
            pltpu.VMEM((72, HALO), jnp.float32),
            pltpu.VMEM((48, 128), jnp.int32),
            pltpu.VMEM((128, 128), jnp.int32),
            pltpu.SMEM((128, 128), jnp.int32),
            pltpu.VMEM((HALF, 128 * PAIRS), jnp.bfloat16),
            pltpu.VMEM((128 * PAIRS, 256), jnp.bfloat16),
            pltpu.SemaphoreType.DMA((4,)),
        ],
        compiler_params=pltpu.CompilerParams(vmem_limit_bytes=40 * 2**20),
        name="conv",
    )(jnp.stack([par, core]).astype(jnp.int32), gather_map, both, outer, w0, w1)
    got = lax.all_to_all(part, "chan", 0, 0, tiled=True).reshape(8, 32, HALF)
    return pl.pallas_call(
        add_kernel,
        out_shape=jax.ShapeDtypeStruct((32, V), jnp.bfloat16),
        in_specs=[vmem],
        out_specs=vmem,
        compiler_params=pltpu.CompilerParams(vmem_limit_bytes=4 * 2**20),
        name="add",
    )(got).T


def solution(mesh):
    in_specs = (P("space", "chan"), P(None, "chan", None), P("space", None, None), P(None, "space"))
    out_specs = P("space", "chan")
    return jax.shard_map(local, mesh=mesh, in_specs=in_specs, out_specs=out_specs, check_vma=False)
```

```python
import jax
import jax.numpy as jnp
from jax import lax
from jax.experimental import pallas as pl
from jax.experimental.pallas import tpu as pltpu
from jax.sharding import PartitionSpec as P

GRID = 8
V = 1024
HALF = V // 2
HALO = 768
OFFS = 27
CENTRE = 13
PAIRS = 14
MSG = 72
ZERO = 9 * V
ROWS = ZERO + 8
FIRST = (3, 5, 0)
STEPS = ((-1, -1), (-1, 0), (-1, 1), (0, -1), (0, 1), (1, -1), (1, 0), (1, 1))


def shift(value, step_row, step_col):
    pairs = [
        (row * GRID + col, (row + step_row) * GRID + col + step_col)
        for row in range(GRID)
        for col in range(GRID)
        if 0 <= row + step_row < GRID and 0 <= col + step_col < GRID
    ]
    return lax.ppermute(value, "space", pairs)


def pick_kernel(where_ref, gm_ref, both_ref, outer_ref,
                lhs, table, digit, lut, comp, index, sem):
    par = where_ref[0]
    core = where_ref[1]
    sources = [both_ref.at[pl.ds(MSG * i, MSG)] for i in range(6)]
    sources += [outer_ref.at[pl.ds(MSG * i, MSG)] for i in range(3)]
    own_base = 3 * core
    base_of = (own_base, jnp.where(core == 0, 6, 0), jnp.where(core == 0, 3, 6))

    for block, source in enumerate(sources):
        digit[8 * block:8 * block + 8, :] = source[64:72, :HALO].astype(jnp.float32)
    for number, (step_row, step_col) in enumerate(STEPS):
        sent = (0, 1, 2)[step_row]
        block = base_of[step_col] + sent
        at = 8 * block + number - FIRST[sent]
        high = digit[pl.ds(at, 1), :]
        low = digit[pl.ds(at + 3, 1), :]
        slot = (high * 32.0 + low).astype(jnp.int32)
        slot = jnp.where(slot >= V, ZERO, slot + block * V)
        for j in range(HALO // 128):
            lut[6 * number + j:6 * number + j + 1, :] = slot[:, 128 * j:128 * (j + 1)]

    def compose(c):
        for k0 in range(0, 32, 8):
            rows = min(8, OFFS - k0)
            here = gm_ref[k0:k0 + rows, pl.ds(pl.multiple_of(par * HALF + 128 * c, 128), 128)]
            if rows < 8:
                here = jnp.concatenate([here, jnp.full((8 - rows, 128), 8 * HALO + V, jnp.int32)], axis=0)
            slot = here - V
            hi = lax.shift_right_arithmetic(slot, 7)
            lo = slot & 127
            got = jnp.where(slot < 0, here + own_base * V, ZERO)
            for t in range(8 * HALO // 128):
                line = jnp.broadcast_to(lut[t:t + 1, :], (8, 128))
                value = jnp.take_along_axis(line, lo, axis=1)
                got = jnp.where(hi == t, value, got)
            comp[32 * c + k0:32 * c + k0 + 8, :] = got
            if rows < 8:
                comp[32 * c + CENTRE:32 * c + CENTRE + 1, :] = got[rows - 1:rows, :]
        rows = pl.ds(32 * c, 32)
        copy = pltpu.make_async_copy(comp.at[rows], index.at[rows], sem.at[c])
        copy.start()
        return copy

    copies = [compose(c) for c in range(HALF // 128)]

    for block, source in enumerate(sources):
        for c in range(V // 128):
            x = source[0:64, 128 * c:128 * (c + 1)].astype(jnp.float32)
            x = jnp.concatenate([x, x], axis=0)
            table[block * V + 128 * c:block * V + 128 * (c + 1), :] = x.T
    table[ZERO:ROWS, :] = jnp.zeros((8, 128), jnp.float32)

    own = pl.multiple_of(own_base * V + par * HALF, 128)
    lhs[:, 128 * (PAIRS - 1):] = table[pl.ds(own, HALF), :].astype(jnp.bfloat16)

    sub = lax.broadcasted_iota(jnp.int32, (8, 128), 0)
    lane = lax.broadcasted_iota(jnp.int32, (8, 128), 1)
    masks = [sub == j for j in range(8)]
    left = lane < 64
    for copy in copies:
        copy.wait()

    @pl.loop(0, 4 * (PAIRS - 1))
    def _(step):
        pair = step >> 2
        quarter = step & 3
        line = quarter * 32 + 2 * pair
        for h in range(0, 128, 16):
            tiles = []
            for g in range(h, h + 16, 8):
                sides = []
                for side in range(2):
                    acc = None
                    for j in range(8):
                        at = index.at[pl.ds(side, 127), pl.ds(g + j, 1)][line, 0]
                        row = table[pl.ds(at, 8, stride=0), :]
                        acc = row if acc is None else jnp.where(masks[j], row, acc)
                    sides.append(acc)
                tiles.append(jnp.where(left, sides[0], sides[1]))
            rows = pl.ds(pl.multiple_of(quarter * 128 + h, 16), 16)
            lanes = pl.ds(pl.multiple_of(128 * pair, 128), 128)
            lhs[rows, lanes] = jnp.concatenate(tiles, axis=0).astype(jnp.bfloat16)


def multiply_kernel(where_ref, lhs, w0_ref, w1_ref, out_ref, wall):
    par = where_ref[0]
    for place in range(OFFS):
        k = {CENTRE: OFFS - 1, OFFS - 1: CENTRE}.get(place, place)
        for side, w_ref in ((par, w0_ref), (1 - par, w1_ref)):
            wall[pl.ds(pl.multiple_of(64 * place + 32 * side, 32), 32), :] = w_ref[32 * k:32 * k + 32, :]
    wall[64 * OFFS:, :] = jnp.zeros((64, 256), jnp.bfloat16)
    total = jnp.dot(lhs[...], wall[...], preferred_element_type=jnp.float32)
    out_ref[...] = total.T


def add_kernel(got_ref, out_ref):
    for half in range(2):
        total = got_ref[half]
        for p in range(1, 4):
            total = total + got_ref[2 * p + half]
        out_ref[:, HALF * half:HALF * (half + 1)] = total.astype(jnp.bfloat16)


def local(features, weights, send_rows, gather_map):
    width = features.shape[1]
    par = lax.axis_index("chan") % 2
    core = lax.axis_index("space") % 2
    flip = [(i, i ^ 1) for i in range(8)]
    duo = [[2 * i, 2 * i + 1] for i in range(4)]
    chips = [[2 * i, 2 * i + 1] for i in range(GRID * GRID // 2)]
    facing = [
        (row * GRID + a, row * GRID + b)
        for row in range(GRID)
        for col in range(1, GRID - 1, 2)
        for a, b in ((col, col + 1), (col + 1, col))
    ]
    w0 = weights.reshape(OFFS * width, 256)
    mine = lax.all_gather(features.T, "chan", axis=0, tiled=True, axis_index_groups=duo)
    rows = jnp.pad(send_rows[0], ((0, 0), (0, V - HALO)))
    high, low = (rows >> 5).astype(jnp.bfloat16), (rows & 31).astype(jnp.bfloat16)
    blank = jnp.zeros((2, V), jnp.bfloat16)

    def message(first):
        return jnp.concatenate([mine, high[first:first + 3], low[first:first + 3], blank], axis=0)

    own = message(FIRST[0])
    up = shift(message(FIRST[1]), 1, 0)
    dn = shift(message(FIRST[2]), -1, 0)
    w1 = lax.ppermute(w0, "chan", flip)
    strip = jnp.concatenate([own, up, dn], axis=0)
    outer = lax.ppermute(strip, "space", facing)
    both = lax.all_gather(strip, "space", axis=0, tiled=True, axis_index_groups=chips)
    vmem = pl.BlockSpec(memory_space=pltpu.VMEM)
    smem = pl.BlockSpec(memory_space=pltpu.SMEM)
    where = jnp.stack([par, core]).astype(jnp.int32)
    lhs = pl.pallas_call(
        pick_kernel,
        out_shape=jax.ShapeDtypeStruct((HALF, 128 * PAIRS), jnp.bfloat16),
        in_specs=[smem] + [vmem] * 3,
        out_specs=vmem,
        scratch_shapes=[
            pltpu.VMEM((ROWS, 128), jnp.float32),
            pltpu.VMEM((72, HALO), jnp.float32),
            pltpu.VMEM((48, 128), jnp.int32),
            pltpu.VMEM((128, 128), jnp.int32),
            pltpu.SMEM((128, 128), jnp.int32),
            pltpu.SemaphoreType.DMA((4,)),
        ],
        compiler_params=pltpu.CompilerParams(vmem_limit_bytes=20 * 2**20),
        cost_estimate=pl.CostEstimate(flops=0, transcendentals=0, bytes_accessed=30 * 2**20),
        name="pick",
    )(where, gather_map, both, outer)
    part = pl.pallas_call(
        multiply_kernel,
        out_shape=jax.ShapeDtypeStruct((256, HALF), jnp.float32),
        in_specs=[smem] + [vmem] * 3,
        out_specs=vmem,
        scratch_shapes=[pltpu.VMEM((128 * PAIRS, 256), jnp.bfloat16)],
        compiler_params=pltpu.CompilerParams(vmem_limit_bytes=16 * 2**20),
        name="multiply",
    )(where, lhs, w0, w1)
    got = lax.all_to_all(part, "chan", 0, 0, tiled=True).reshape(8, 32, HALF)
    return pl.pallas_call(
        add_kernel,
        out_shape=jax.ShapeDtypeStruct((32, V), jnp.bfloat16),
        in_specs=[vmem],
        out_specs=vmem,
        compiler_params=pltpu.CompilerParams(vmem_limit_bytes=4 * 2**20),
        name="add",
    )(got).T


def solution(mesh):
    in_specs = (P("space", "chan"), P(None, "chan", None), P("space", None, None), P(None, "space"))
    out_specs = P("space", "chan")
    return jax.shard_map(local, mesh=mesh, in_specs=in_specs, out_specs=out_specs, check_vma=False)
```

```python
import functools

import jax
import jax.numpy as jnp
from jax import lax
from jax.experimental import pallas as pl
from jax.experimental.pallas import tpu as pltpu
from jax.sharding import PartitionSpec as P

GRID = 8
V = 1024
HALF = V // 2
HALO = 768
OFFS = 27
CENTRE = 13
PAIRS = 14
MSG = 72
ZERO = 9 * V
ROWS = ZERO + 8
FIRST = (3, 5, 0)
STEPS = ((-1, -1), (-1, 0), (-1, 1), (0, -1), (0, 1), (1, -1), (1, 0), (1, 1))


def shift(value, step_row, step_col):
    pairs = [
        (row * GRID + col, (row + step_row) * GRID + col + step_col)
        for row in range(GRID)
        for col in range(GRID)
        if 0 <= row + step_row < GRID and 0 <= col + step_col < GRID
    ]
    return lax.ppermute(value, "space", pairs)


def conv_kernel(par_ref, core_ref, gm_ref, both_ref, outer_ref, w0_ref, w1_ref,
                out_ref, table, digit, lut, comp, index, lhs, wall, sem):
    par = par_ref[0]
    core = core_ref[0]
    sources = [both_ref.at[pl.ds(MSG * i, MSG)] for i in range(6)]
    sources += [outer_ref.at[pl.ds(MSG * i, MSG)] for i in range(3)]
    own_base = 3 * core
    base_of = (own_base, jnp.where(core == 0, 6, 0), jnp.where(core == 0, 3, 6))

    for block, source in enumerate(sources):
        digit[8 * block:8 * block + 8, :] = source[64:72, :HALO].astype(jnp.float32)
    for number, (step_row, step_col) in enumerate(STEPS):
        sent = (0, 1, 2)[step_row]
        block = base_of[step_col] + sent
        at = 8 * block + number - FIRST[sent]
        high = digit[pl.ds(at, 1), :]
        low = digit[pl.ds(at + 3, 1), :]
        slot = (high * 32.0 + low).astype(jnp.int32)
        slot = jnp.where(slot >= V, ZERO, slot + block * V)
        for j in range(HALO // 128):
            lut[6 * number + j:6 * number + j + 1, :] = slot[:, 128 * j:128 * (j + 1)]

    def compose(c):
        for k0 in range(0, 32, 8):
            rows = min(8, OFFS - k0)
            here = gm_ref[k0:k0 + rows, pl.ds(pl.multiple_of(par * HALF + 128 * c, 128), 128)]
            if rows < 8:
                here = jnp.concatenate([here, jnp.full((8 - rows, 128), 8 * HALO + V, jnp.int32)], axis=0)
            slot = here - V
            hi = lax.shift_right_arithmetic(slot, 7)
            lo = slot & 127
            got = jnp.where(slot < 0, here + own_base * V, ZERO)
            for t in range(8 * HALO // 128):
                line = jnp.broadcast_to(lut[t:t + 1, :], (8, 128))
                value = jnp.take_along_axis(line, lo, axis=1)
                got = jnp.where(hi == t, value, got)
            comp[32 * c + k0:32 * c + k0 + 8, :] = got
            if rows < 8:
                comp[32 * c + CENTRE:32 * c + CENTRE + 1, :] = got[rows - 1:rows, :]
        rows = pl.ds(32 * c, 32)
        copy = pltpu.make_async_copy(comp.at[rows], index.at[rows], sem.at[c])
        copy.start()
        return copy

    copies = [compose(c) for c in range(HALF // 128)]

    for block, source in enumerate(sources):
        for c in range(V // 128):
            x = source[0:64, 128 * c:128 * (c + 1)].astype(jnp.float32)
            x = jnp.concatenate([x, x], axis=0)
            table[block * V + 128 * c:block * V + 128 * (c + 1), :] = x.T
    table[ZERO:ROWS, :] = jnp.zeros((8, 128), jnp.float32)

    for place in range(OFFS):
        k = {CENTRE: OFFS - 1, OFFS - 1: CENTRE}.get(place, place)
        for side, w_ref in ((par, w0_ref), (1 - par, w1_ref)):
            wall[pl.ds(pl.multiple_of(64 * place + 32 * side, 32), 32), :] = w_ref[32 * k:32 * k + 32, :]
    wall[64 * OFFS:, :] = jnp.zeros((64, 256), jnp.bfloat16)

    own = pl.multiple_of(own_base * V + par * HALF, 128)
    lhs[:, 128 * (PAIRS - 1):] = table[pl.ds(own, HALF), :].astype(jnp.bfloat16)

    sub = lax.broadcasted_iota(jnp.int32, (8, 128), 0)
    lane = lax.broadcasted_iota(jnp.int32, (8, 128), 1)
    masks = [sub == j for j in range(8)]
    left = lane < 64
    def pick(pair, quarter):
        lanes = pl.ds(128 * pair, 128)
        line = 2 * pair
        for h in range(0, 128, 16):
            tiles = []
            for g in range(h, h + 16, 8):
                sides = []
                for side in range(2):
                    acc = None
                    for j in range(8):
                        at = index.at[pl.ds(32 * quarter + side, 31), pl.ds(g + j, 1)][line, 0]
                        row = table[pl.ds(at, 8, stride=0), :]
                        acc = row if acc is None else jnp.where(masks[j], row, acc)
                    sides.append(acc)
                tiles.append(jnp.where(left, sides[0], sides[1]))
            rows = slice(128 * quarter + h, 128 * quarter + h + 16)
            lhs[rows, lanes] = jnp.concatenate(tiles, axis=0).astype(jnp.bfloat16)

    for quarter, copy in enumerate(copies):
        copy.wait()
        for pair in range(PAIRS - 1):
            pick(pair, quarter)

    total = jnp.dot(lhs[...], wall[...], preferred_element_type=jnp.float32)
    out_ref[...] = total.T


def add_kernel(got_ref, out_ref):
    for half in range(2):
        total = got_ref[half]
        for p in range(1, 4):
            total = total + got_ref[2 * p + half]
        out_ref[:, HALF * half:HALF * (half + 1)] = total.astype(jnp.bfloat16)


def local(features, weights, send_rows, gather_map):
    width = features.shape[1]
    par = lax.axis_index("chan") % 2
    core = lax.axis_index("space") % 2
    flip = [(i, i ^ 1) for i in range(8)]
    duo = [[2 * i, 2 * i + 1] for i in range(4)]
    chips = [[2 * i, 2 * i + 1] for i in range(GRID * GRID // 2)]
    facing = [
        (row * GRID + a, row * GRID + b)
        for row in range(GRID)
        for col in range(1, GRID - 1, 2)
        for a, b in ((col, col + 1), (col + 1, col))
    ]
    w0 = weights.reshape(OFFS * width, 256)
    mine = lax.all_gather(features.T, "chan", axis=0, tiled=True, axis_index_groups=duo)
    rows = jnp.pad(send_rows[0], ((0, 0), (0, V - HALO)))
    high, low = (rows >> 5).astype(jnp.bfloat16), (rows & 31).astype(jnp.bfloat16)
    blank = jnp.zeros((2, V), jnp.bfloat16)

    def message(first):
        return jnp.concatenate([mine, high[first:first + 3], low[first:first + 3], blank], axis=0)

    own = message(FIRST[0])
    up = shift(message(FIRST[1]), 1, 0)
    dn = shift(message(FIRST[2]), -1, 0)
    w1 = lax.ppermute(w0, "chan", flip)
    strip = jnp.concatenate([own, up, dn], axis=0)
    outer = lax.ppermute(strip, "space", facing)
    both = lax.all_gather(strip, "space", axis=0, tiled=True, axis_index_groups=chips)
    vmem = pl.BlockSpec(memory_space=pltpu.VMEM)
    part = pl.pallas_call(
        conv_kernel,
        out_shape=jax.ShapeDtypeStruct((256, HALF), jnp.float32),
        in_specs=[pl.BlockSpec(memory_space=pltpu.SMEM)] * 2 + [vmem] * 5,
        out_specs=vmem,
        scratch_shapes=[
            pltpu.VMEM((ROWS, 128), jnp.float32),
            pltpu.VMEM((72, HALO), jnp.float32),
            pltpu.VMEM((48, 128), jnp.int32),
            pltpu.VMEM((128, 128), jnp.int32),
            pltpu.SMEM((128, 128), jnp.int32),
            pltpu.VMEM((HALF, 128 * PAIRS), jnp.bfloat16),
            pltpu.VMEM((128 * PAIRS, 256), jnp.bfloat16),
            pltpu.SemaphoreType.DMA((4,)),
        ],
        compiler_params=pltpu.CompilerParams(vmem_limit_bytes=40 * 2**20),
        name="conv",
    )(par.reshape(1), core.reshape(1), gather_map, both, outer, w0, w1)
    got = lax.all_to_all(part, "chan", 0, 0, tiled=True).reshape(8, 32, HALF)
    return pl.pallas_call(
        add_kernel,
        out_shape=jax.ShapeDtypeStruct((32, V), jnp.bfloat16),
        in_specs=[vmem],
        out_specs=vmem,
        compiler_params=pltpu.CompilerParams(vmem_limit_bytes=4 * 2**20),
        name="add",
    )(got).T


def solution(mesh):
    in_specs = (P("space", "chan"), P(None, "chan", None), P("space", None, None), P(None, "space"))
    out_specs = P("space", "chan")
    return jax.shard_map(local, mesh=mesh, in_specs=in_specs, out_specs=out_specs, check_vma=False)
```

```python
import functools

import jax
import jax.numpy as jnp
from jax import lax
from jax.experimental import pallas as pl
from jax.experimental.pallas import tpu as pltpu
from jax.sharding import PartitionSpec as P

GRID = 8
V = 1024
HALF = V // 2
HALO = 768
OFFS = 27
CENTRE = 13
PAIRS = 14
MSG = 72
ZERO = 9 * V
ROWS = ZERO + 8
FIRST = (3, 5, 0)
STEPS = ((-1, -1), (-1, 0), (-1, 1), (0, -1), (0, 1), (1, -1), (1, 0), (1, 1))


def shift(value, step_row, step_col):
    pairs = [
        (row * GRID + col, (row + step_row) * GRID + col + step_col)
        for row in range(GRID)
        for col in range(GRID)
        if 0 <= row + step_row < GRID and 0 <= col + step_col < GRID
    ]
    return lax.ppermute(value, "space", pairs)


def pick_kernel(par_ref, core_ref, gm_ref, both_ref, outer_ref,
                lhs, table, digit, lut, comp, index, sem):
    par = par_ref[0]
    core = core_ref[0]
    sources = [both_ref.at[pl.ds(MSG * i, MSG)] for i in range(6)]
    sources += [outer_ref.at[pl.ds(MSG * i, MSG)] for i in range(3)]
    own_base = 3 * core
    base_of = (own_base, jnp.where(core == 0, 6, 0), jnp.where(core == 0, 3, 6))

    for block, source in enumerate(sources):
        digit[8 * block:8 * block + 8, :] = source[64:72, :HALO].astype(jnp.float32)
    for number, (step_row, step_col) in enumerate(STEPS):
        sent = (0, 1, 2)[step_row]
        block = base_of[step_col] + sent
        at = 8 * block + number - FIRST[sent]
        high = digit[pl.ds(at, 1), :]
        low = digit[pl.ds(at + 3, 1), :]
        slot = (high * 32.0 + low).astype(jnp.int32)
        slot = jnp.where(slot >= V, ZERO, slot + block * V)
        for j in range(HALO // 128):
            lut[6 * number + j:6 * number + j + 1, :] = slot[:, 128 * j:128 * (j + 1)]

    def compose(c):
        for k0 in range(0, 32, 8):
            rows = min(8, OFFS - k0)
            here = gm_ref[k0:k0 + rows, pl.ds(pl.multiple_of(par * HALF + 128 * c, 128), 128)]
            if rows < 8:
                here = jnp.concatenate([here, jnp.full((8 - rows, 128), 8 * HALO + V, jnp.int32)], axis=0)
            slot = here - V
            hi = lax.shift_right_arithmetic(slot, 7)
            lo = slot & 127
            got = jnp.where(slot < 0, here + own_base * V, ZERO)
            for t in range(8 * HALO // 128):
                line = jnp.broadcast_to(lut[t:t + 1, :], (8, 128))
                value = jnp.take_along_axis(line, lo, axis=1)
                got = jnp.where(hi == t, value, got)
            comp[32 * c + k0:32 * c + k0 + 8, :] = got
            if rows < 8:
                comp[32 * c + CENTRE:32 * c + CENTRE + 1, :] = got[rows - 1:rows, :]
        rows = pl.ds(32 * c, 32)
        copy = pltpu.make_async_copy(comp.at[rows], index.at[rows], sem.at[c])
        copy.start()
        return copy

    copies = [compose(c) for c in range(HALF // 128)]

    for block, source in enumerate(sources):
        for c in range(V // 128):
            x = source[0:64, 128 * c:128 * (c + 1)].astype(jnp.float32)
            x = jnp.concatenate([x, x], axis=0)
            table[block * V + 128 * c:block * V + 128 * (c + 1), :] = x.T
    table[ZERO:ROWS, :] = jnp.zeros((8, 128), jnp.float32)

    own = pl.multiple_of(own_base * V + par * HALF, 128)
    lhs[:, 128 * (PAIRS - 1):] = table[pl.ds(own, HALF), :].astype(jnp.bfloat16)

    sub = lax.broadcasted_iota(jnp.int32, (8, 128), 0)
    lane = lax.broadcasted_iota(jnp.int32, (8, 128), 1)
    masks = [sub == j for j in range(8)]
    left = lane < 64
    def pick(pair, quarter):
        lanes = pl.ds(128 * pair, 128)
        line = 2 * pair
        for h in range(0, 128, 16):
            tiles = []
            for g in range(h, h + 16, 8):
                sides = []
                for side in range(2):
                    acc = None
                    for j in range(8):
                        at = index.at[pl.ds(32 * quarter + side, 31), pl.ds(g + j, 1)][line, 0]
                        row = table[pl.ds(at, 8, stride=0), :]
                        acc = row if acc is None else jnp.where(masks[j], row, acc)
                    sides.append(acc)
                tiles.append(jnp.where(left, sides[0], sides[1]))
            rows = slice(128 * quarter + h, 128 * quarter + h + 16)
            lhs[rows, lanes] = jnp.concatenate(tiles, axis=0).astype(jnp.bfloat16)

    for quarter, copy in enumerate(copies):
        copy.wait()
        for pair in range(PAIRS - 1):
            pick(pair, quarter)


def multiply_kernel(par_ref, lhs, w0_ref, w1_ref, out_ref, wall):
    par = par_ref[0]
    for place in range(OFFS):
        k = {CENTRE: OFFS - 1, OFFS - 1: CENTRE}.get(place, place)
        for side, w_ref in ((par, w0_ref), (1 - par, w1_ref)):
            wall[pl.ds(pl.multiple_of(64 * place + 32 * side, 32), 32), :] = w_ref[32 * k:32 * k + 32, :]
    wall[64 * OFFS:, :] = jnp.zeros((64, 256), jnp.bfloat16)
    total = jnp.dot(lhs[...], wall[...], preferred_element_type=jnp.float32)
    out_ref[...] = total.T


def add_kernel(got_ref, out_ref):
    for half in range(2):
        total = got_ref[half]
        for p in range(1, 4):
            total = total + got_ref[2 * p + half]
        out_ref[:, HALF * half:HALF * (half + 1)] = total.astype(jnp.bfloat16)


def local(features, weights, send_rows, gather_map):
    width = features.shape[1]
    par = lax.axis_index("chan") % 2
    core = lax.axis_index("space") % 2
    flip = [(i, i ^ 1) for i in range(8)]
    duo = [[2 * i, 2 * i + 1] for i in range(4)]
    chips = [[2 * i, 2 * i + 1] for i in range(GRID * GRID // 2)]
    facing = [
        (row * GRID + a, row * GRID + b)
        for row in range(GRID)
        for col in range(1, GRID - 1, 2)
        for a, b in ((col, col + 1), (col + 1, col))
    ]
    w0 = weights.reshape(OFFS * width, 256)
    mine = lax.all_gather(features.T, "chan", axis=0, tiled=True, axis_index_groups=duo)
    rows = jnp.pad(send_rows[0], ((0, 0), (0, V - HALO)))
    high, low = (rows >> 5).astype(jnp.bfloat16), (rows & 31).astype(jnp.bfloat16)
    blank = jnp.zeros((2, V), jnp.bfloat16)

    def message(first):
        return jnp.concatenate([mine, high[first:first + 3], low[first:first + 3], blank], axis=0)

    own = message(FIRST[0])
    up = shift(message(FIRST[1]), 1, 0)
    dn = shift(message(FIRST[2]), -1, 0)
    w1 = lax.ppermute(jnp.pad(w0, ((0, 96), (0, 0))), "chan", flip)
    strip = jnp.concatenate([own, up, dn], axis=0)
    outer = lax.ppermute(strip, "space", facing)
    both = lax.all_gather(strip, "space", axis=0, tiled=True, axis_index_groups=chips)
    vmem = pl.BlockSpec(memory_space=pltpu.VMEM)
    smem = pl.BlockSpec(memory_space=pltpu.SMEM)
    lhs = pl.pallas_call(
        pick_kernel,
        out_shape=jax.ShapeDtypeStruct((HALF, 128 * PAIRS), jnp.bfloat16),
        in_specs=[smem] * 2 + [vmem] * 3,
        out_specs=vmem,
        scratch_shapes=[
            pltpu.VMEM((ROWS, 128), jnp.float32),
            pltpu.VMEM((72, HALO), jnp.float32),
            pltpu.VMEM((48, 128), jnp.int32),
            pltpu.VMEM((128, 128), jnp.int32),
            pltpu.SMEM((128, 128), jnp.int32),
            pltpu.SemaphoreType.DMA((4,)),
        ],
        compiler_params=pltpu.CompilerParams(vmem_limit_bytes=20 * 2**20),
        cost_estimate=pl.CostEstimate(flops=0, transcendentals=0, bytes_accessed=1024),
        name="pick",
    )(par.reshape(1), core.reshape(1), gather_map, both, outer)
    part = pl.pallas_call(
        multiply_kernel,
        out_shape=jax.ShapeDtypeStruct((256, HALF), jnp.float32),
        in_specs=[smem] + [vmem] * 3,
        out_specs=vmem,
        scratch_shapes=[pltpu.VMEM((128 * PAIRS, 256), jnp.bfloat16)],
        compiler_params=pltpu.CompilerParams(vmem_limit_bytes=16 * 2**20),
        name="multiply",
    )(par.reshape(1), lhs, w0, w1)
    got = lax.all_to_all(part, "chan", 0, 0, tiled=True).reshape(8, 32, HALF)
    return pl.pallas_call(
        add_kernel,
        out_shape=jax.ShapeDtypeStruct((32, V), jnp.bfloat16),
        in_specs=[vmem],
        out_specs=vmem,
        compiler_params=pltpu.CompilerParams(vmem_limit_bytes=4 * 2**20),
        name="add",
    )(got).T


def solution(mesh):
    in_specs = (P("space", "chan"), P(None, "chan", None), P("space", None, None), P(None, "space"))
    out_specs = P("space", "chan")
    return jax.shard_map(local, mesh=mesh, in_specs=in_specs, out_specs=out_specs, check_vma=False)
```

```python
import functools

import jax
import jax.numpy as jnp
from jax import lax
from jax.experimental import pallas as pl
from jax.experimental.pallas import tpu as pltpu
from jax.sharding import PartitionSpec as P

GRID = 8
V = 1024
HALF = V // 2
HALO = 768
OFFS = 27
CENTRE = 13
PAIRS = 14
MSG = 72
ZERO = 9 * V
ROWS = ZERO + 8
FIRST = (3, 5, 0)
STEPS = ((-1, -1), (-1, 0), (-1, 1), (0, -1), (0, 1), (1, -1), (1, 0), (1, 1))


def shift(value, step_row, step_col):
    pairs = [
        (row * GRID + col, (row + step_row) * GRID + col + step_col)
        for row in range(GRID)
        for col in range(GRID)
        if 0 <= row + step_row < GRID and 0 <= col + step_col < GRID
    ]
    return lax.ppermute(value, "space", pairs)


def pick_kernel(par_ref, core_ref, gm_ref, both_ref, outer_ref,
                lhs, table, digit, lut, comp, index, sem):
    par = par_ref[0]
    core = core_ref[0]
    sources = [both_ref.at[pl.ds(MSG * i, MSG)] for i in range(6)]
    sources += [outer_ref.at[pl.ds(64 * i, 64)] for i in range(3)]
    own_base = 3 * core
    base_of = (own_base, jnp.where(core == 0, 6, 0), jnp.where(core == 0, 3, 6))

    for block, source in enumerate(sources[:6]):
        digit[8 * block:8 * block + 8, :] = source[64:72, :HALO].astype(jnp.float32)
    face = outer_ref[192:200, :HALO].astype(jnp.float32)
    for i in range(6):
        at = 48 + 8 * (i // 2) + 3 * (i % 2)
        digit[at:at + 3, :] = jnp.broadcast_to(face[i:i + 1], (3, HALO))
    for number, (step_row, step_col) in enumerate(STEPS):
        sent = (0, 1, 2)[step_row]
        block = base_of[step_col] + sent
        at = 8 * block + number - FIRST[sent]
        high = digit[pl.ds(at, 1), :]
        low = digit[pl.ds(at + 3, 1), :]
        slot = (high * 32.0 + low).astype(jnp.int32)
        slot = jnp.where(slot >= V, ZERO, slot + block * V)
        for j in range(HALO // 128):
            lut[6 * number + j:6 * number + j + 1, :] = slot[:, 128 * j:128 * (j + 1)]

    def compose(c):
        for k0 in range(0, 32, 8):
            rows = min(8, OFFS - k0)
            here = gm_ref[k0:k0 + rows, pl.ds(pl.multiple_of(par * HALF + 128 * c, 128), 128)]
            if rows < 8:
                here = jnp.concatenate([here, jnp.full((8 - rows, 128), 8 * HALO + V, jnp.int32)], axis=0)
            slot = here - V
            hi = lax.shift_right_arithmetic(slot, 7)
            lo = slot & 127
            got = jnp.where(slot < 0, here + own_base * V, ZERO)
            for t in range(8 * HALO // 128):
                line = jnp.broadcast_to(lut[t:t + 1, :], (8, 128))
                value = jnp.take_along_axis(line, lo, axis=1)
                got = jnp.where(hi == t, value, got)
            comp[32 * c + k0:32 * c + k0 + 8, :] = got
            if rows < 8:
                comp[32 * c + CENTRE:32 * c + CENTRE + 1, :] = got[rows - 1:rows, :]
        rows = pl.ds(32 * c, 32)
        copy = pltpu.make_async_copy(comp.at[rows], index.at[rows], sem.at[c])
        copy.start()
        return copy

    copies = [compose(c) for c in range(HALF // 128)]

    for block, source in enumerate(sources):
        for c in range(V // 128):
            x = source[0:64, 128 * c:128 * (c + 1)].astype(jnp.float32)
            x = jnp.concatenate([x, x], axis=0)
            table[block * V + 128 * c:block * V + 128 * (c + 1), :] = x.T
    table[ZERO:ROWS, :] = jnp.zeros((8, 128), jnp.float32)

    own = pl.multiple_of(own_base * V + par * HALF, 128)
    lhs[:, 128 * (PAIRS - 1):] = table[pl.ds(own, HALF), :].astype(jnp.bfloat16)

    sub = lax.broadcasted_iota(jnp.int32, (8, 128), 0)
    lane = lax.broadcasted_iota(jnp.int32, (8, 128), 1)
    masks = [sub == j for j in range(8)]
    left = lane < 64
    def pick(pair, quarter):
        lanes = pl.ds(128 * pair, 128)
        line = 2 * pair
        for h in range(0, 128, 16):
            tiles = []
            for g in range(h, h + 16, 8):
                sides = []
                for side in range(2):
                    acc = None
                    for j in range(8):
                        at = index.at[pl.ds(32 * quarter + side, 31), pl.ds(g + j, 1)][line, 0]
                        row = table[pl.ds(at, 8, stride=0), :]
                        acc = row if acc is None else jnp.where(masks[j], row, acc)
                    sides.append(acc)
                tiles.append(jnp.where(left, sides[0], sides[1]))
            rows = slice(128 * quarter + h, 128 * quarter + h + 16)
            lhs[rows, lanes] = jnp.concatenate(tiles, axis=0).astype(jnp.bfloat16)

    for quarter, copy in enumerate(copies):
        copy.wait()
        for pair in range(PAIRS - 1):
            pick(pair, quarter)


def multiply_kernel(par_ref, lhs, w0_ref, w1_ref, out_ref, wall):
    par = par_ref[0]
    for place in range(OFFS):
        k = {CENTRE: OFFS - 1, OFFS - 1: CENTRE}.get(place, place)
        for side, w_ref in ((par, w0_ref), (1 - par, w1_ref)):
            wall[pl.ds(pl.multiple_of(64 * place + 32 * side, 32), 32), :] = w_ref[32 * k:32 * k + 32, :]
    wall[64 * OFFS:, :] = jnp.zeros((64, 256), jnp.bfloat16)
    total = jnp.dot(lhs[...], wall[...], preferred_element_type=jnp.float32)
    out_ref[...] = total.T


def add_kernel(got_ref, out_ref):
    for half in range(2):
        total = got_ref[half]
        for p in range(1, 4):
            total = total + got_ref[2 * p + half]
        out_ref[:, HALF * half:HALF * (half + 1)] = total.astype(jnp.bfloat16)


def local(features, weights, send_rows, gather_map):
    width = features.shape[1]
    par = lax.axis_index("chan") % 2
    core = lax.axis_index("space") % 2
    flip = [(i, i ^ 1) for i in range(8)]
    duo = [[2 * i, 2 * i + 1] for i in range(4)]
    chips = [[2 * i, 2 * i + 1] for i in range(GRID * GRID // 2)]
    facing = [
        (row * GRID + a, row * GRID + b)
        for row in range(GRID)
        for col in range(1, GRID - 1, 2)
        for a, b in ((col, col + 1), (col + 1, col))
    ]
    w0 = weights.reshape(OFFS * width, 256)
    mine = lax.all_gather(features.T, "chan", axis=0, tiled=True, axis_index_groups=duo)
    rows = jnp.pad(send_rows[0], ((0, 0), (0, V - HALO)))
    high, low = (rows >> 5).astype(jnp.bfloat16), (rows & 31).astype(jnp.bfloat16)
    blank = jnp.zeros((2, V), jnp.bfloat16)

    def message(first):
        return jnp.concatenate([mine, high[first:first + 3], low[first:first + 3], blank], axis=0)

    own = message(FIRST[0])
    up = shift(message(FIRST[1]), 1, 0)
    dn = shift(message(FIRST[2]), -1, 0)
    w1 = lax.ppermute(w0, "chan", flip)
    strip = jnp.concatenate([own, up, dn], axis=0)
    faces = [
        jnp.concatenate([b[64 + t + i:65 + t + i] for b, t in zip((own, up, dn), at) for i in (0, 3)], axis=0)
        for at in ((0, 0, 0), (1, 2, 2))
    ]
    face = jnp.where(core == 0, faces[0], faces[1])
    outer = jnp.concatenate([own[:64], up[:64], dn[:64], face, blank], axis=0)
    outer = lax.ppermute(outer, "space", facing)
    both = lax.all_gather(strip, "space", axis=0, tiled=True, axis_index_groups=chips)
    vmem = pl.BlockSpec(memory_space=pltpu.VMEM)
    smem = pl.BlockSpec(memory_space=pltpu.SMEM)
    lhs = pl.pallas_call(
        pick_kernel,
        out_shape=jax.ShapeDtypeStruct((HALF, 128 * PAIRS), jnp.bfloat16),
        in_specs=[smem] * 2 + [vmem] * 3,
        out_specs=vmem,
        scratch_shapes=[
            pltpu.VMEM((ROWS, 128), jnp.float32),
            pltpu.VMEM((72, HALO), jnp.float32),
            pltpu.VMEM((48, 128), jnp.int32),
            pltpu.VMEM((128, 128), jnp.int32),
            pltpu.SMEM((128, 128), jnp.int32),
            pltpu.SemaphoreType.DMA((4,)),
        ],
        compiler_params=pltpu.CompilerParams(vmem_limit_bytes=20 * 2**20),
        cost_estimate=pl.CostEstimate(flops=0, transcendentals=0, bytes_accessed=1024),
        name="pick",
    )(par.reshape(1), core.reshape(1), gather_map, both, outer)
    part = pl.pallas_call(
        multiply_kernel,
        out_shape=jax.ShapeDtypeStruct((256, HALF), jnp.float32),
        in_specs=[smem] + [vmem] * 3,
        out_specs=vmem,
        scratch_shapes=[pltpu.VMEM((128 * PAIRS, 256), jnp.bfloat16)],
        compiler_params=pltpu.CompilerParams(vmem_limit_bytes=16 * 2**20),
        name="multiply",
    )(par.reshape(1), lhs, w0, w1)
    got = lax.all_to_all(part, "chan", 0, 0, tiled=True).reshape(8, 32, HALF)
    return pl.pallas_call(
        add_kernel,
        out_shape=jax.ShapeDtypeStruct((32, V), jnp.bfloat16),
        in_specs=[vmem],
        out_specs=vmem,
        compiler_params=pltpu.CompilerParams(vmem_limit_bytes=4 * 2**20),
        name="add",
    )(got).T


def solution(mesh):
    in_specs = (P("space", "chan"), P(None, "chan", None), P("space", None, None), P(None, "space"))
    out_specs = P("space", "chan")
    return jax.shard_map(local, mesh=mesh, in_specs=in_specs, out_specs=out_specs, check_vma=False)
```
